128 devices in a mesh: dp: 8 (over x_lo, y), ctx: 16 (over x_hi, z, core).
Axes of the slice: x: 4 (x_hi: 2, x_lo: 2; x = x_hi * 2 + x_lo), y: 4, z: 4, core: 2. Of those that a mesh axis runs over, the one named last changes fastest.
Arguments:
- enc_feat: bfloat16 [8, 256, 16, 512], P(None, ('dp', 'ctx')), may hold values from -6 to 6
- conv_w: bfloat16 [3, 512, 64], replicated, may hold values from -0.15625 to 0.15625
- w_lat: bfloat16 [64, 3072], replicated, may hold values from -0.75 to 0.75
- q_raw: bfloat16 [8, 4096, 3072], P('dp', 'ctx'), may hold values from -40 to 40
- k_raw: bfloat16 [8, 4096, 3072], P('dp', 'ctx'), may hold values from -40 to 40
- v_in: bfloat16 [8, 4096, 3072], P('dp', 'ctx'), may hold values from -6 to 6
- valid: int32 [8, 16], P('dp', 'ctx'), may hold values from 128 to 256, as said below
- d_out: bfloat16 [8, 4096, 3072], P('dp', 'ctx'), may hold values from -6 to 6
Outputs:
- attn_out: bfloat16 [8, 4096, 3072], P('dp', 'ctx')
- dq: bfloat16 [8, 4096, 3072], P('dp', 'ctx')
- dk: bfloat16 [8, 4096, 3072], P('dp', 'ctx')
- dv: bfloat16 [8, 4096, 3072], P('dp', 'ctx')
- dw_lat: float32 [64, 3072], replicated
The draws below stay inside these ranges and needn't reach their ends.
Inputs may be any that keep to these rules, and one draw needn't show every extreme that they name: `valid`: the first stretch of every clip is full.
All inputs are finite; a program needn't handle non-finite values.
Results may differ from the reference program's by a relative error of at most 0.03.
Values may be sent and summed in bfloat16 or wider, within the bound.
A program may use at most 128 MiB of HBM per device.

```python
import math
import jax
import jax.numpy as jnp
from jax import lax

DH = 128
CE = 512
LAT = 64
BACK = 4
STRETCH = 256
HD = 3072
CLIPS = 8
STRETCHES = 16
TOKENS = 4096
PIX = 16
FRAMES = 256


def query_key_pair(key):
    shape = (CLIPS, TOKENS, HD)
    queries = jax.random.normal(jax.random.fold_in(key, 101), shape, jnp.float32)
    keys = jax.random.normal(jax.random.fold_in(key, 202), shape, jnp.float32)
    return (jnp.clip(queries, -40.0, 40.0), jnp.clip(keys, -40.0, 40.0))


def draw_q_raw(key, part):
    return query_key_pair(key)[0].astype(jnp.bfloat16)


def draw_k_raw(key, part):
    return query_key_pair(key)[1].astype(jnp.bfloat16)


def draw_valid(key, part):
    counts = jax.random.randint(key, (CLIPS, STRETCHES), STRETCH // 2, STRETCH + 1, jnp.int32)
    first = jnp.arange(STRETCHES, dtype=jnp.int32)[None, :] == 0
    return jnp.where(first, jnp.int32(STRETCH), counts).astype(jnp.int32)


def level_of(key, extent, split, least, top_value):
    factor_of, own = 1.0, jax.random.fold_in(key, 6)
    for dim, shards_of in split:
        draws = jnp.exp(jax.random.uniform(jax.random.fold_in(own, dim), (shards_of,), jnp.float32, least / len(split), top_value / len(split)))
        factor_of = factor_of * jnp.repeat(draws, extent[dim] // shards_of).reshape([-1 if axis == dim else 1 for axis in range(len(extent))])
    return factor_of


def bell_draw(rng, extent, scale, most, shards=(), kind=jnp.bfloat16):
    loudness = level_of(rng, extent, shards, -0.22, 0.18) if shards else 1.0
    array = jax.random.normal(rng, extent, jnp.float32) * scale * loudness
    return jnp.minimum(jnp.maximum(array, -most), most).astype(kind)


def setup_inputs(seed: int = 0) -> dict:
    key_of = jax.random.split(jax.random.key(seed), 9)
    return {
        "enc_feat": bell_draw(key_of[0], (CLIPS, FRAMES, PIX, CE), 1.0, 6.0, ((1, 128),)),
        "conv_w": bell_draw(key_of[1], (3, CE, LAT), (3 * CE) ** -0.5, 0.15625),
        "w_lat": bell_draw(key_of[2], (LAT, HD), LAT ** -0.5, 0.75),
        "q_raw": draw_q_raw(jax.random.fold_in(key_of[8], 71), 0),
        "k_raw": draw_k_raw(jax.random.fold_in(key_of[8], 71), 0),
        "v_in": bell_draw(key_of[5], (CLIPS, TOKENS, HD), 1.0, 6.0, ((0, 8), (1, 16))),
        "valid": draw_valid(jax.random.fold_in(key_of[8], 71), 0),
        "d_out": bell_draw(key_of[7], (CLIPS, TOKENS, HD), 1.0, 6.0, ((0, 8), (1, 16))),
    }


def rounded(values):
    return lax.optimization_barrier(values.astype(jnp.bfloat16)).astype(jnp.float32)

def attend(query, keys, vals, grads, allowed):
    count = query.shape[0]
    width = keys.shape[0]
    scale = 1.0 / math.sqrt(DH)
    query_heads = query.astype(jnp.float32).reshape(count, -1, DH)
    key_heads = keys.astype(jnp.float32).reshape(width, -1, DH)
    value_heads = vals.astype(jnp.float32).reshape(width, -1, DH)
    grad_heads = grads.astype(jnp.float32).reshape(count, -1, DH)
    scores = jnp.einsum('qhd,khd->hqk', query_heads, key_heads) * scale
    scores = jnp.where(allowed[None, None, :], scores, -1e+30)
    highest = lax.optimization_barrier(jnp.max(scores, axis=-1, keepdims=True))
    expo = jnp.exp(scores - highest)
    probs = expo / lax.optimization_barrier(jnp.sum(expo, axis=-1, keepdims=True))
    probs_low = rounded(probs)
    output = jnp.einsum('hqk,khd->qhd', probs_low, value_heads).astype(jnp.bfloat16)
    grad_probs = jnp.einsum('qhd,khd->hqk', grad_heads, value_heads)
    delta = jnp.einsum('qhd,qhd->hq', grad_heads, output.astype(jnp.float32))
    grad_scores = rounded(probs * (grad_probs - delta[:, :, None]) * scale)
    dquery = jnp.einsum('hqk,khd->qhd', grad_scores, key_heads).astype(jnp.bfloat16)
    dkeys = jnp.einsum('hqk,qhd->khd', grad_scores, query_heads).astype(jnp.bfloat16)
    dvals = jnp.einsum('hqk,qhd->khd', probs_low, grad_heads).astype(jnp.bfloat16)
    return (output.reshape(count, -1), dquery.reshape(count, -1), dkeys.reshape(width, -1), dvals.reshape(width, -1))

def reference(enc_feat, conv_w, w_lat, q_raw, k_raw, v_in, valid, d_out):
    frame_count = enc_feat.shape[1]
    padded = jnp.pad(enc_feat, ((0, 0), (2, 0), (0, 0), (0, 0)))
    latent = jnp.zeros((CLIPS, frame_count, PIX, LAT), jnp.float32)
    for tap_index in range(3):
        window_feat = padded[:, 2 - tap_index:2 - tap_index + frame_count].astype(jnp.float32)
        latent = latent + jnp.einsum('cfpe,el->cfpl', window_feat, conv_w[tap_index].astype(jnp.float32))
    lat_tokens = latent.astype(jnp.bfloat16).reshape(CLIPS, TOKENS, LAT)
    values = (v_in.astype(jnp.float32) + jnp.einsum('ctl,lh->cth', lat_tokens.astype(jnp.float32), w_lat.astype(jnp.float32))).astype(jnp.bfloat16)
    positions = jnp.arange(TOKENS, dtype=jnp.int32)
    key_ok = (positions % STRETCH)[None, :] < jnp.repeat(valid, STRETCH, axis=1)
    margin = BACK * STRETCH
    keys_padded = jnp.pad(k_raw, ((0, 0), (margin, 0), (0, 0)))
    values_padded = jnp.pad(values, ((0, 0), (margin, 0), (0, 0)))
    ok_padded = jnp.pad(key_ok, ((0, 0), (margin, 0)))

    def per_clip(operands):
        query_clip, key_clip, value_clip, ok_clip, grad_clip = operands

        def step(carry, stretch_index):
            key_total, value_total = carry
            start = (stretch_index * STRETCH).astype(jnp.int32)
            span = (BACK + 1) * STRETCH
            query_block = lax.dynamic_slice_in_dim(query_clip, start, STRETCH, 0)
            grad_block = lax.dynamic_slice_in_dim(grad_clip, start, STRETCH, 0)
            key_block = lax.dynamic_slice_in_dim(key_clip, start, span, 0)
            value_block = lax.dynamic_slice_in_dim(value_clip, start, span, 0)
            ok_block = lax.dynamic_slice_in_dim(ok_clip, start, span, 0)
            output, dquery, dkeys, dvals = attend(query_block, key_block, value_block, grad_block, ok_block)
            key_total = lax.dynamic_update_slice_in_dim(key_total, lax.dynamic_slice_in_dim(key_total, start, span, 0) + dkeys.astype(jnp.float32), start, 0)
            value_total = lax.dynamic_update_slice_in_dim(value_total, lax.dynamic_slice_in_dim(value_total, start, span, 0) + dvals.astype(jnp.float32), start, 0)
            return ((key_total, value_total), (output, dquery))
        zeros_total = jnp.zeros((TOKENS + margin, HD), jnp.float32)
        (key_total, value_total), (outputs, dqueries) = lax.scan(step, (zeros_total, zeros_total), jnp.arange(STRETCHES, dtype=jnp.int32))
        return (outputs.reshape(TOKENS, HD), dqueries.reshape(TOKENS, HD), key_total[margin:].astype(jnp.bfloat16), value_total[margin:].astype(jnp.bfloat16))
    attn_out, dq, dk, dv = lax.map(per_clip, (q_raw, keys_padded, values_padded, ok_padded, d_out))
    dw_lat = jnp.einsum('ctl,cth->lh', lat_tokens.astype(jnp.float32), dv.astype(jnp.float32))
    return (attn_out, dq, dk, dv, dw_lat)
```

```python
import math

import jax
import jax.numpy as jnp
from jax import lax
from jax.experimental import pallas as pl
from jax.experimental.pallas import tpu as pltpu
from jax.sharding import PartitionSpec as P

MESH = pl.DeviceIdType.MESH
DH = 128
ROWS = 256
GROUP = 8
HEADS = 3
BACK = 4
HALO = BACK * ROWS
OWN = GROUP * ROWS
SPAN = (BACK + 1) * ROWS
SCALE = 1.0 / math.sqrt(DH)
EXP2 = SCALE * math.log2(math.e)
MASKED = -1e30
F32 = jnp.float32
BF16 = jnp.bfloat16


def last_last(a, b):
    return lax.dot_general(a, b, (((1,), (1,)), ((), ())), preferred_element_type=F32)


def first_first(a, b):
    return lax.dot_general(a, b, (((0,), (0,)), ((), ())), preferred_element_type=F32)


def dot(a, b):
    return jnp.dot(a, b, preferred_element_type=F32)


def kernel(
    valid_ref, feat_ref, wcat_ref, wlat_ref, q_ref, k_ref, v_ref, do_ref,
    out_ref, dq_ref, dk_ref, dv_ref, dw_ref,
    qb, dob, kb, vb, acc_k, acc_v, stg, part_out, part_in, bias, vbuf, w2, lbuf,
    pk_out, pk_in, dwp, rsb, agb, plb,
    in_s, in_r, fin_s, fin_r, halo_s, halo_r, part_s, part_r, val_s, val_r,
    lat_s, lat_r, enc_s, enc_r, rs_s, rs_r, ag_s, ag_r, pl_s, pl_r, loc,
):
    dp = lax.axis_index("dp")
    ctx = lax.axis_index("ctx")
    xhi = ctx // GROUP
    g = ctx % GROUP
    first = xhi == 0
    partner = (dp, ctx + GROUP - 2 * GROUP * xhi)
    slab_stretch = dp * 2 + xhi
    next_stretch = (slab_stretch + 1) % 16
    self_main = ctx == slab_stretch
    self_carry = ctx == next_stretch
    last_slab = g == GROUP - 1

    def remote(src, dst, ss, rs, dev):
        return pltpu.make_async_remote_copy(
            src_ref=src, dst_ref=dst, send_sem=ss, recv_sem=rs, device_id=dev,
            device_id_type=MESH)

    def local(src, dst, sem):
        return pltpu.make_async_copy(src, dst, sem)

    def await_bytes(ref, sem):
        pltpu.make_async_copy(ref, ref, sem).wait()

    def peer(n):
        return (g + n) % GROUP

    def group_dev(p):
        return (dp, xhi * GROUP + p)

    def loop(lo, hi, body):
        lax.fori_loop(lo, hi, lambda i, c: (body(i), c)[1], 0)

    barrier = pltpu.get_barrier_semaphore()

    def signal(dev):
        pl.semaphore_signal(barrier, inc=1, device_id=dev, device_id_type=MESH)

    loop(1, GROUP, lambda n: signal(group_dev(peer(n))))

    def plane_dev(n):
        m = (dp * 2 + xhi + n) % 16
        return (m // 2, (m % 2) * GROUP + g)

    loop(1, 16, lambda n: signal(plane_dev(n)))
    src_dp = ctx // 2
    src_ctx = (ctx % 2) * GROUP

    def signal_source(i):
        @pl.when(jnp.logical_or(src_dp != dp, src_ctx + i != ctx))
        def _():
            signal((src_dp, src_ctx + i))

    loop(0, GROUP, signal_source)
    prev = (ctx + 15) % 16
    prev_dp = prev // 2
    prev_ctx = (prev % 2) * GROUP + GROUP - 1

    @pl.when(jnp.logical_or(prev_dp != dp, prev_ctx != ctx))
    def _():
        signal((prev_dp, prev_ctx))

    one = jnp.int32(1)
    zero = jnp.int32(0)
    expected = (
        (GROUP - 1) + 15 + 8 - jnp.where(self_main, one, zero)
        + jnp.where(last_slab, 8 - jnp.where(self_carry, one, zero), zero)
    )

    local(wlat_ref.at[:, pl.ds(pl.multiple_of(g * HEADS * DH, DH), HEADS * DH)],
          w2.at[pl.ds(64, 64)], loc.at[0]).start()
    a4 = dot(feat_ref[...], wcat_ref[:, 0:128]).reshape(8, 2, 16, 128)
    b4 = dot(feat_ref[...], wcat_ref[:, 128:256]).reshape(8, 2, 16, 128)
    mix = a4[:, 1] + b4[:, 0]
    low = lax.broadcasted_iota(jnp.int32, (8, 16, 128), 2) < 64
    pk_out[:, 0:16, :] = jnp.where(low, a4[:, 0], mix)
    pk_out[:, 16:32, :] = jnp.where(low, mix, b4[:, 1])

    pl.semaphore_wait(barrier, expected)

    def main_copy(c):
        return remote(pk_out.at[c], pk_in.at[1 + g], enc_s.at[0, c], enc_r.at[0],
                      (c, slab_stretch))

    def carry_copy(c):
        return remote(pk_out.at[c], pk_in.at[0], enc_s.at[1, c], enc_r.at[0],
                      (c, next_stretch))

    def is_self(c, own):
        return jnp.logical_and(own, c == dp)

    def send_main(c):
        @pl.when(is_self(c, self_main))
        def _():
            local(pk_out.at[c], pk_in.at[1 + g], enc_r.at[0]).start()

        @pl.when(jnp.logical_not(is_self(c, self_main)))
        def _():
            main_copy(c).start()

    def send_carry(c):
        @pl.when(is_self(c, self_carry))
        def _():
            local(pk_out.at[c], pk_in.at[0], enc_r.at[0]).start()

        @pl.when(jnp.logical_not(is_self(c, self_carry)))
        def _():
            carry_copy(c).start()

    loop(0, 8, send_main)

    @pl.when(last_slab)
    def _():
        loop(0, 8, send_carry)

    local(valid_ref, vbuf.at[BACK + g], val_r.at[0]).start()
    loop(1, GROUP, lambda n: remote(
        valid_ref, vbuf.at[BACK + g], val_s.at[0], val_r.at[0],
        group_dev(peer(n))).start())

    arrays = ((k_ref, kb, HALO), (q_ref, qb, 0), (do_ref, dob, 0), (v_ref, vb, HALO))

    def send_head(h):
        for a, (src, buf, off) in enumerate(arrays):
            dst = buf.at[h, pl.ds(pl.multiple_of(off + g * ROWS, ROWS), ROWS)]

            def cols(p):
                return src.at[:, pl.ds(pl.multiple_of((HEADS * p + h) * DH, DH), DH)]

            local(cols(g), dst, in_r.at[h, a]).start()
            loop(1, GROUP, lambda n: remote(
                cols(peer(n)), dst, in_s.at[h, a], in_r.at[h, a],
                group_dev(peer(n))).start())

    send_head(0)

    w2[0:64, :] = jnp.zeros((64, HEADS * DH), BF16)
    w2[128:192, :] = jnp.zeros((64, HEADS * DH), BF16)

    @pl.when(first)
    def _():
        kb[:, 0:HALO, :] = jnp.zeros((HEADS, HALO, DH), BF16)
        vb[:, 0:HALO, :] = jnp.zeros((HEADS, HALO, DH), BF16)
        vbuf[0:BACK] = jnp.zeros((BACK, 8, 128), jnp.int32)

    await_bytes(pk_in, enc_r.at[0])
    before = jnp.concatenate(
        [jnp.where(ctx == 0, jnp.zeros((1, 32, 128), F32), pk_in[0:1]), pk_in[1:8]], axis=0)
    x = (pk_in[1:9] + pltpu.roll(before, 64, 2)).reshape(ROWS, 128)
    lat_low = lax.broadcasted_iota(jnp.int32, (128, 128), 1) < 64
    lbuf[g] = jnp.where(lat_low, x[0:128], pltpu.roll(x[128:256], 64, 1)).astype(BF16)
    loop(1, GROUP, lambda n: remote(
        lbuf.at[g], lbuf.at[g], lat_s.at[0], lat_r.at[0], group_dev(peer(n))).start())

    send_head(1)
    send_head(2)

    await_bytes(vbuf.at[BACK:], val_r.at[0])
    halo_valid = remote(vbuf.at[pl.ds(GROUP, BACK)], vbuf.at[pl.ds(0, BACK)],
                        val_s.at[1], val_r.at[1], partner)

    @pl.when(first)
    def _():
        halo_valid.start()

    @pl.when(jnp.logical_not(first))
    def _():
        await_bytes(vbuf.at[0:BACK], val_r.at[1])

    def make_bias(s):
        rows = lax.broadcasted_iota(jnp.int32, (ROWS, 128), 0)
        ok = rows < vbuf[s, 0:1, :]
        col = jnp.where(ok, jnp.zeros((ROWS, 128), F32), jnp.full((ROWS, 128), MASKED, F32))
        at = pl.ds(pl.multiple_of(s * ROWS, ROWS), ROWS)
        bias[at, 0:128] = col
        bias[at, 128:256] = col

    loop(0, BACK + GROUP, make_bias)
    local(wlat_ref.at[:, pl.ds(0, HEADS * DH)], w2.at[pl.ds(64, 64)], loc.at[0]).wait()
    await_bytes(lbuf.at[0:GROUP - 1], lat_r.at[0])

    def halo_copy(h, a):
        buf = (kb, vb)[a]
        return remote(buf.at[h, pl.ds(OWN, HALO)], buf.at[h, pl.ds(0, HALO)],
                      halo_s.at[h, a], halo_r.at[h, a], partner)

    def part_copy(h):
        return remote(part_out.at[h], part_in.at[h], part_s.at[h], part_r.at[h], partner)

    def send_result(h, a, s):
        ref = (out_ref, dq_ref, dk_ref, dv_ref)[a]
        src = stg.at[a, h, pl.ds(pl.multiple_of(s * ROWS, ROWS), ROWS)]
        dst = ref.at[:, pl.ds(pl.multiple_of((HEADS * g + h) * DH, DH), DH)]

        @pl.when(s == g)
        def _():
            local(src, dst, fin_r.at[a]).start()

        @pl.when(s != g)
        def _():
            remote(src, dst, fin_s.at[h, a], fin_r.at[a], group_dev(s)).start()

    def stretch(h, i):
        rows = pl.ds(pl.multiple_of(i * ROWS, ROWS), ROWS)
        span = pl.ds(pl.multiple_of(i * ROWS, ROWS), SPAN)
        q = qb[h, rows]
        do = dob[h, rows]
        keys = kb[h, span]
        vals = vb[h, span]
        s = last_last(keys, q) + bias[span, :]
        m = jnp.max(s, axis=0, keepdims=True)
        e = jnp.exp2((s - m) * EXP2)
        p = e * (1.0 / jnp.sum(e, axis=0, keepdims=True))
        p_low = p.astype(BF16)
        out_t = first_first(vals, p_low)
        out = out_t.T.astype(BF16)
        stg[0, h, rows] = out
        delta = jnp.sum(do.astype(F32).T * out_t.astype(BF16).astype(F32), axis=0, keepdims=True)
        grad = last_last(vals, do)
        ds = (p * (grad - delta)).astype(BF16)
        stg[1, h, rows] = (first_first(keys, ds) * SCALE).T.astype(BF16)
        acc_k[h, span] += dot(ds, q)
        acc_v[h, span] += dot(p_low, do)
        send_result(h, 0, i)
        send_result(h, 1, i)

    def finish(h, s, with_part):
        rows = pl.ds(pl.multiple_of(HALO + s * ROWS, ROWS), ROWS)
        dk = acc_k[h, rows] * SCALE
        dv = acc_v[h, rows]
        if with_part:
            at = pl.ds(pl.multiple_of((s - BACK) * ROWS, ROWS), ROWS)
            dk = dk + part_in[h, 0, at].astype(F32)
            dv = dv + part_in[h, 1, at].astype(F32)
        own = pl.ds(pl.multiple_of(s * ROWS, ROWS), ROWS)
        stg[2, h, own] = dk.astype(BF16)
        stg[3, h, own] = dv.astype(BF16)
        send_result(h, 2, s)
        send_result(h, 3, s)

    def owner_of(h):
        return h % 2

    def rs_copy(h, j):
        return remote(
            dwp.at[h, pl.ds(pl.multiple_of(8 * j, 8), 8)], rsb.at[h, dp * 2 + xhi],
            rs_s.at[h, j], rs_r.at[h], (j, owner_of(h) * GROUP + g))

    def rs_self(h, j):
        return jnp.logical_and(j == dp, xhi == owner_of(h))

    def late(h):
        @pl.when(first)
        def _():
            await_bytes(part_in.at[h], part_r.at[h])
            loop(BACK, GROUP, lambda s: finish(h, s, True))

        def add(s, carry):
            top, bottom = carry
            at = pl.multiple_of(s * ROWS, ROWS)
            lat = lbuf[s]
            top = top + first_first(lat, stg[3, h, pl.ds(at, 128)])
            bottom = bottom + first_first(lat, stg[3, h, pl.ds(at + 128, 128)])
            return top, bottom

        zeros = jnp.zeros((128, 128), F32)
        top, bottom = lax.fori_loop(0, GROUP, add, (zeros, zeros))
        dwp[h] = top[0:64] + bottom[64:128]

        def send(j):
            @pl.when(rs_self(h, j))
            def _():
                local(dwp.at[h, pl.ds(pl.multiple_of(8 * j, 8), 8)],
                      rsb.at[h, dp * 2 + xhi], rs_r.at[h]).start()

            @pl.when(jnp.logical_not(rs_self(h, j)))
            def _():
                rs_copy(h, j).start()

        loop(0, 8, send)

    def head(h):
        for a, (_, buf, off) in enumerate(arrays):
            await_bytes(buf.at[h, pl.ds(off, OWN)], in_r.at[h, a])

        def add_latents(s):
            lat = lbuf[s]
            at = pl.multiple_of(HALO + s * ROWS, ROWS)
            cols = pl.ds(pl.multiple_of(h * DH, DH), DH)
            upper = pl.ds(at, 128)
            lower = pl.ds(at + 128, 128)
            vb[h, upper] = (vb[h, upper].astype(F32) + dot(lat, w2[64:192, cols])).astype(BF16)
            vb[h, lower] = (vb[h, lower].astype(F32) + dot(lat, w2[0:128, cols])).astype(BF16)

        @pl.when(first)
        def _():
            halo_copy(h, 0).start()

        loop(0, GROUP, add_latents)

        @pl.when(first)
        def _():
            halo_copy(h, 1).start()

        acc_k[h] = jnp.zeros((HALO + OWN, DH), F32)
        acc_v[h] = jnp.zeros((HALO + OWN, DH), F32)

        loop(BACK, GROUP, lambda i: stretch(h, i))

        @pl.when(jnp.logical_not(first))
        def _():
            await_bytes(kb.at[h, pl.ds(0, HALO)], halo_r.at[h, 0])
            await_bytes(vb.at[h, pl.ds(0, HALO)], halo_r.at[h, 1])

        loop(0, BACK, lambda i: stretch(h, i))

        @pl.when(jnp.logical_not(first))
        def _():
            part_out[h, 0] = (acc_k[h, 0:HALO] * SCALE).astype(BF16)
            part_out[h, 1] = acc_v[h, 0:HALO].astype(BF16)
            part_copy(h).start()

        loop(0, BACK, lambda s: finish(h, s, False))

        @pl.when(jnp.logical_not(first))
        def _():
            loop(BACK, GROUP, lambda s: finish(h, s, False))

        @pl.when(h > 0)
        def _():
            late(h - 1)

    loop(0, HEADS, head)

    def ag_copy(h, n):
        return remote(agb.at[h, g], agb.at[h, g], ag_s.at[h], ag_r.at[h], group_dev(peer(n)))

    def spread(h):
        @pl.when(xhi == owner_of(h))
        def _():
            await_bytes(rsb.at[h], rs_r.at[h])
            agb[h, g] = jnp.sum(rsb[h], axis=0)
            loop(1, GROUP, lambda n: ag_copy(h, n).start())
            await_bytes(agb.at[h, 0:GROUP - 1], ag_r.at[h])
            local(agb.at[h], plb.at[h * 8 + dp], pl_r.at[h]).start()
            loop(1, 16, lambda n: remote(
                agb.at[h], plb.at[h * 8 + dp], pl_s.at[h], pl_r.at[h], plane_dev(n)).start())

    spread(0)
    spread(1)
    late(2)
    spread(2)

    def assemble(h):
        await_bytes(plb.at[pl.ds(h * 8, 8)], pl_r.at[h])
        for j in range(8):
            for p in range(GROUP):
                dw_ref[8 * j:8 * j + 8, (HEADS * p + h) * DH:(HEADS * p + h + 1) * DH] = (
                    plb[h * 8 + j, p])

    for h in range(HEADS):
        assemble(h)

    for a, ref in enumerate((out_ref, dq_ref, dk_ref, dv_ref)):
        await_bytes(ref, fin_r.at[a])

    def wait_main(c):
        @pl.when(jnp.logical_not(is_self(c, self_main)))
        def _():
            main_copy(c).wait_send()

    def wait_carry(c):
        @pl.when(jnp.logical_not(is_self(c, self_carry)))
        def _():
            carry_copy(c).wait_send()

    loop(0, 8, wait_main)

    @pl.when(last_slab)
    def _():
        loop(0, 8, wait_carry)

    await_bytes(vbuf.at[0:GROUP - 1], val_s.at[0])
    await_bytes(lbuf.at[0:GROUP - 1], lat_s.at[0])

    @pl.when(first)
    def _():
        await_bytes(vbuf.at[0:BACK], val_s.at[1])

    def drain(h):
        for a in range(4):
            await_bytes(qb.at[h, pl.ds(0, OWN - ROWS)], in_s.at[h, a])
            await_bytes(stg.at[a, h, pl.ds(0, OWN - ROWS)], fin_s.at[h, a])

        @pl.when(first)
        def _():
            await_bytes(kb.at[h, pl.ds(0, HALO)], halo_s.at[h, 0])
            await_bytes(vb.at[h, pl.ds(0, HALO)], halo_s.at[h, 1])

        @pl.when(jnp.logical_not(first))
        def _():
            await_bytes(part_out.at[h], part_s.at[h])

        def wait_rs(j):
            @pl.when(jnp.logical_not(rs_self(h, j)))
            def _():
                rs_copy(h, j).wait_send()

        loop(0, 8, wait_rs)

        @pl.when(xhi == owner_of(h))
        def _():
            await_bytes(agb.at[h, 0:GROUP - 1], ag_s.at[h])
            await_bytes(plb.at[0:15], pl_s.at[h])

    loop(0, HEADS, drain)


def on_device(enc_feat, conv_w, w_lat, q_raw, k_raw, v_in, valid, d_out):
    feat = enc_feat.reshape(ROWS, enc_feat.shape[3])
    wcat = jnp.concatenate([conv_w[0], conv_w[1], conv_w[1], conv_w[2]], axis=1)
    valid_tile = jnp.broadcast_to(valid, (8, 128))
    result = jax.ShapeDtypeStruct((ROWS, q_raw.shape[2]), BF16)
    anywhere = pl.BlockSpec(memory_space=pl.ANY)
    vmem = pl.BlockSpec(memory_space=pltpu.VMEM)
    dma = pltpu.SemaphoreType.DMA
    out, dq, dk, dv, dw = pl.pallas_call(
        kernel,
        out_shape=(result, result, result, result,
                   jax.ShapeDtypeStruct(w_lat.shape, F32)),
        in_specs=[vmem, vmem, vmem] + [anywhere] * 5,
        out_specs=(anywhere,) * 4 + (vmem,),
        scratch_shapes=[
            pltpu.VMEM((HEADS, OWN, DH), BF16),
            pltpu.VMEM((HEADS, OWN, DH), BF16),
            pltpu.VMEM((HEADS, HALO + OWN, DH), BF16),
            pltpu.VMEM((HEADS, HALO + OWN, DH), BF16),
            pltpu.VMEM((HEADS, HALO + OWN, DH), F32),
            pltpu.VMEM((HEADS, HALO + OWN, DH), F32),
            pltpu.VMEM((4, HEADS, OWN, DH), BF16),
            pltpu.VMEM((HEADS, 2, HALO, DH), BF16),
            pltpu.VMEM((HEADS, 2, HALO, DH), BF16),
            pltpu.VMEM((HALO + OWN, ROWS), F32),
            pltpu.VMEM((BACK + GROUP, 8, 128), jnp.int32),
            pltpu.VMEM((192, HEADS * DH), BF16),
            pltpu.VMEM((GROUP, 128, 128), BF16),
            pltpu.VMEM((8, 32, 128), F32),
            pltpu.VMEM((9, 32, 128), F32),
            pltpu.VMEM((HEADS, 64, 128), F32),
            pltpu.VMEM((HEADS, 16, 8, 128), F32),
            pltpu.VMEM((HEADS, GROUP, 8, 128), F32),
            pltpu.VMEM((HEADS * 8, GROUP, 8, 128), F32),
            dma((HEADS, 4)), dma((HEADS, 4)),
            dma((HEADS, 4)), dma((4,)),
            dma((HEADS, 2)), dma((HEADS, 2)),
            dma((HEADS,)), dma((HEADS,)),
            dma((2,)), dma((2,)),
            dma((1,)), dma((1,)),
            dma((2, 8)), dma((1,)),
            dma((HEADS, 8)), dma((HEADS,)),
            dma((HEADS,)), dma((HEADS,)),
            dma((HEADS,)), dma((HEADS,)),
            dma((1,)),
        ],
        name="slab_attention",
        compiler_params=pltpu.CompilerParams(
            collective_id=0, has_side_effects=True, vmem_limit_bytes=60 * 1024 * 1024),
    )(valid_tile, feat, wcat, w_lat, q_raw[0], k_raw[0], v_in[0], d_out[0])
    return out[None], dq[None], dk[None], dv[None], dw


def solution(mesh):
    tokens = P("dp", "ctx", None)
    return jax.shard_map(
        on_device,
        mesh=mesh,
        in_specs=(P(None, ("dp", "ctx"), None, None), P(), P(), tokens, tokens, tokens,
                  P("dp", "ctx"), tokens),
        out_specs=(tokens, tokens, tokens, tokens, P()),
        check_vma=False,
    )
```

```python
import math

import jax
import jax.numpy as jnp
from jax import lax
from jax.experimental import pallas as pl
from jax.experimental.pallas import tpu as pltpu
from jax.sharding import PartitionSpec as P

MESH = pl.DeviceIdType.MESH
DH = 128
ROWS = 256
GROUP = 8
HEADS = 3
BACK = 4
HALO = BACK * ROWS
OWN = GROUP * ROWS
SPAN = (BACK + 1) * ROWS
SCALE = 1.0 / math.sqrt(DH)
EXP2 = SCALE * math.log2(math.e)
MASKED = -1e30
F32 = jnp.float32
BF16 = jnp.bfloat16


def last_last(a, b):
    return lax.dot_general(a, b, (((1,), (1,)), ((), ())), preferred_element_type=F32)


def first_first(a, b):
    return lax.dot_general(a, b, (((0,), (0,)), ((), ())), preferred_element_type=F32)


def dot(a, b):
    return jnp.dot(a, b, preferred_element_type=F32)


def kernel(
    count_ref, feat_ref, taps_ref, wlat_ref, q_ref, k_ref, v_ref, do_ref,
    out_ref, dq_ref, dk_ref, dv_ref, dw_ref,
    qb, dob, kb, vb, acc_k, acc_v, stg, part_out, part_in, bias, vbuf, valid_ref, w2, lbuf,
    pk_out, pk_in, dwp, rsb, agb, plb,
    in_s, in_r, fin_s, fin_r, halo_s, halo_r, part_s, part_r, val_s, val_r,
    lat_s, lat_r, enc_s, enc_r, rs_s, rs_r, ag_s, ag_r, pl_s, pl_r, loc,
):
    dp = lax.axis_index("dp")
    ctx = lax.axis_index("ctx")
    xhi = ctx // GROUP
    g = ctx % GROUP
    first = xhi == 0
    partner = (dp, ctx + GROUP - 2 * GROUP * xhi)
    slab_stretch = dp * 2 + xhi
    next_stretch = (slab_stretch + 1) % 16
    self_main = ctx == slab_stretch
    self_carry = ctx == next_stretch
    last_slab = g == GROUP - 1

    def remote(src, dst, ss, rs, dev):
        return pltpu.make_async_remote_copy(
            src_ref=src, dst_ref=dst, send_sem=ss, recv_sem=rs, device_id=dev,
            device_id_type=MESH)

    def local(src, dst, sem):
        return pltpu.make_async_copy(src, dst, sem)

    def await_bytes(ref, sem):
        pltpu.make_async_copy(ref, ref, sem).wait()

    def peer(n):
        return (g + n) % GROUP

    def group_dev(p):
        return (dp, xhi * GROUP + p)

    def loop(lo, hi, body):
        lax.fori_loop(lo, hi, lambda i, c: (body(i), c)[1], 0)

    barrier = pltpu.get_barrier_semaphore()

    def signal(dev):
        pl.semaphore_signal(barrier, inc=1, device_id=dev, device_id_type=MESH)

    loop(1, GROUP, lambda n: signal(group_dev(peer(n))))

    def plane_dev(n):
        m = (dp * 2 + xhi + n) % 16
        return (m // 2, (m % 2) * GROUP + g)

    loop(1, 16, lambda n: signal(plane_dev(n)))
    src_dp = ctx // 2
    src_ctx = (ctx % 2) * GROUP

    def signal_source(i):
        @pl.when(jnp.logical_or(src_dp != dp, src_ctx + i != ctx))
        def _():
            signal((src_dp, src_ctx + i))

    loop(0, GROUP, signal_source)
    prev = (ctx + 15) % 16
    prev_dp = prev // 2
    prev_ctx = (prev % 2) * GROUP + GROUP - 1

    @pl.when(jnp.logical_or(prev_dp != dp, prev_ctx != ctx))
    def _():
        signal((prev_dp, prev_ctx))

    one = jnp.int32(1)
    zero = jnp.int32(0)
    expected = (
        (GROUP - 1) + 15 + 8 - jnp.where(self_main, one, zero)
        + jnp.where(last_slab, 8 - jnp.where(self_carry, one, zero), zero)
    )

    local(wlat_ref.at[:, pl.ds(pl.multiple_of(g * HEADS * DH, DH), HEADS * DH)],
          w2.at[pl.ds(64, 64)], loc.at[0]).start()
    valid_ref[...] = jnp.full((8, 128), count_ref[0, 0], jnp.int32)
    a4 = last_last(feat_ref[...], taps_ref[0:128]).reshape(8, 2, 16, 128)
    b4 = last_last(feat_ref[...], taps_ref[64:192]).reshape(8, 2, 16, 128)
    mix = a4[:, 1] + b4[:, 0]
    low = lax.broadcasted_iota(jnp.int32, (8, 16, 128), 2) < 64
    pk_out[:, 0:16, :] = jnp.where(low, a4[:, 0], mix)
    pk_out[:, 16:32, :] = jnp.where(low, mix, b4[:, 1])

    pl.semaphore_wait(barrier, expected)

    def main_copy(c):
        return remote(pk_out.at[c], pk_in.at[1 + g], enc_s.at[0, c], enc_r.at[0],
                      (c, slab_stretch))

    def carry_copy(c):
        return remote(pk_out.at[c], pk_in.at[0], enc_s.at[1, c], enc_r.at[0],
                      (c, next_stretch))

    def is_self(c, own):
        return jnp.logical_and(own, c == dp)

    def send_main(c):
        @pl.when(is_self(c, self_main))
        def _():
            local(pk_out.at[c], pk_in.at[1 + g], enc_r.at[0]).start()

        @pl.when(jnp.logical_not(is_self(c, self_main)))
        def _():
            main_copy(c).start()

    def send_carry(c):
        @pl.when(is_self(c, self_carry))
        def _():
            local(pk_out.at[c], pk_in.at[0], enc_r.at[0]).start()

        @pl.when(jnp.logical_not(is_self(c, self_carry)))
        def _():
            carry_copy(c).start()

    loop(0, 8, send_main)

    @pl.when(last_slab)
    def _():
        loop(0, 8, send_carry)

    local(valid_ref, vbuf.at[BACK + g], val_r.at[0]).start()
    loop(1, GROUP, lambda n: remote(
        valid_ref, vbuf.at[BACK + g], val_s.at[0], val_r.at[0],
        group_dev(peer(n))).start())

    arrays = ((k_ref, kb, HALO), (q_ref, qb, 0), (do_ref, dob, 0), (v_ref, vb, HALO))

    def send_head(h):
        for a, (src, buf, off) in enumerate(arrays):
            dst = buf.at[h, pl.ds(pl.multiple_of(off + g * ROWS, ROWS), ROWS)]

            def cols(p):
                return src.at[:, pl.ds(pl.multiple_of((HEADS * p + h) * DH, DH), DH)]

            local(cols(g), dst, in_r.at[h, a]).start()
            loop(1, GROUP, lambda n: remote(
                cols(peer(n)), dst, in_s.at[h, a], in_r.at[h, a],
                group_dev(peer(n))).start())

    send_head(0)

    w2[0:64, :] = jnp.zeros((64, HEADS * DH), BF16)
    w2[128:192, :] = jnp.zeros((64, HEADS * DH), BF16)

    @pl.when(first)
    def _():
        kb[:, 0:HALO, :] = jnp.zeros((HEADS, HALO, DH), BF16)
        vb[:, 0:HALO, :] = jnp.zeros((HEADS, HALO, DH), BF16)
        vbuf[0:BACK] = jnp.zeros((BACK, 8, 128), jnp.int32)

    await_bytes(pk_in, enc_r.at[0])
    before = jnp.concatenate(
        [jnp.where(ctx == 0, jnp.zeros((1, 32, 128), F32), pk_in[0:1]), pk_in[1:8]], axis=0)
    x = (pk_in[1:9] + pltpu.roll(before, 64, 2)).reshape(ROWS, 128)
    lat_low = lax.broadcasted_iota(jnp.int32, (128, 128), 1) < 64
    lbuf[g] = jnp.where(lat_low, x[0:128], pltpu.roll(x[128:256], 64, 1)).astype(BF16)
    loop(1, GROUP, lambda n: remote(
        lbuf.at[g], lbuf.at[g], lat_s.at[0], lat_r.at[0], group_dev(peer(n))).start())

    send_head(1)
    send_head(2)

    await_bytes(vbuf.at[BACK:], val_r.at[0])
    halo_valid = remote(vbuf.at[pl.ds(GROUP, BACK)], vbuf.at[pl.ds(0, BACK)],
                        val_s.at[1], val_r.at[1], partner)

    @pl.when(first)
    def _():
        halo_valid.start()

    @pl.when(jnp.logical_not(first))
    def _():
        await_bytes(vbuf.at[0:BACK], val_r.at[1])

    def make_bias(s):
        rows = lax.broadcasted_iota(jnp.int32, (ROWS, 128), 0)
        ok = rows < vbuf[s, 0:1, :]
        col = jnp.where(ok, jnp.zeros((ROWS, 128), F32), jnp.full((ROWS, 128), MASKED, F32))
        at = pl.ds(pl.multiple_of(s * ROWS, ROWS), ROWS)
        bias[at, 0:128] = col
        bias[at, 128:256] = col

    loop(0, BACK + GROUP, make_bias)
    local(wlat_ref.at[:, pl.ds(0, HEADS * DH)], w2.at[pl.ds(64, 64)], loc.at[0]).wait()
    await_bytes(lbuf.at[0:GROUP - 1], lat_r.at[0])

    def halo_copy(h, a):
        buf = (kb, vb)[a]
        return remote(buf.at[h, pl.ds(OWN, HALO)], buf.at[h, pl.ds(0, HALO)],
                      halo_s.at[h, a], halo_r.at[h, a], partner)

    def part_copy(h):
        return remote(part_out.at[h], part_in.at[h], part_s.at[h], part_r.at[h], partner)

    def send_result(h, a, s):
        ref = (out_ref, dq_ref, dk_ref, dv_ref)[a]
        src = stg.at[a, h, pl.ds(pl.multiple_of(s * ROWS, ROWS), ROWS)]
        dst = ref.at[:, pl.ds(pl.multiple_of((HEADS * g + h) * DH, DH), DH)]

        @pl.when(s == g)
        def _():
            local(src, dst, fin_r.at[a]).start()

        @pl.when(s != g)
        def _():
            remote(src, dst, fin_s.at[h, a], fin_r.at[a], group_dev(s)).start()

    def stretch(h, i):
        rows = pl.ds(pl.multiple_of(i * ROWS, ROWS), ROWS)
        span = pl.ds(pl.multiple_of(i * ROWS, ROWS), SPAN)
        q = qb[h, rows]
        do = dob[h, rows]
        keys = kb[h, span]
        vals = vb[h, span]
        s = last_last(keys, q) + bias[span, :]
        m = jnp.max(s, axis=0, keepdims=True)
        e = jnp.exp2((s - m) * EXP2)
        p = e * (1.0 / jnp.sum(e, axis=0, keepdims=True))
        p_low = p.astype(BF16)
        out_t = first_first(vals, p_low)
        out = out_t.T.astype(BF16)
        stg[0, h, rows] = out
        delta = jnp.sum(do.astype(F32).T * out_t.astype(BF16).astype(F32), axis=0, keepdims=True)
        grad = last_last(vals, do)
        ds = (p * (grad - delta)).astype(BF16)
        stg[1, h, rows] = (first_first(keys, ds) * SCALE).T.astype(BF16)
        acc_k[h, span] += dot(ds, q)
        acc_v[h, span] += dot(p_low, do)
        send_result(h, 0, i)
        send_result(h, 1, i)

    def send_sums(h, s):
        send_result(h, 2, s)
        send_result(h, 3, s)

    def finish(h, s, with_part):
        rows = pl.ds(pl.multiple_of(HALO + s * ROWS, ROWS), ROWS)
        dk = acc_k[h, rows] * SCALE
        dv = acc_v[h, rows]
        if with_part:
            at = pl.ds(pl.multiple_of((s - BACK) * ROWS, ROWS), ROWS)
            dk = dk + part_in[h, 0, at].astype(F32)
            dv = dv + part_in[h, 1, at].astype(F32)
        own = pl.ds(pl.multiple_of(s * ROWS, ROWS), ROWS)
        stg[2, h, own] = dk.astype(BF16)
        stg[3, h, own] = dv.astype(BF16)

        @pl.when(h < HEADS - 1)
        def _():
            send_sums(h, s)

    def owner_of(h):
        return h % 2

    def rs_copy(h, j):
        return remote(
            dwp.at[h, pl.ds(pl.multiple_of(8 * j, 8), 8)], rsb.at[h, dp * 2 + xhi],
            rs_s.at[h, j], rs_r.at[h], (j, owner_of(h) * GROUP + g))

    def rs_self(h, j):
        return jnp.logical_and(j == dp, xhi == owner_of(h))

    def late(h):
        @pl.when(first)
        def _():
            await_bytes(part_in.at[h], part_r.at[h])
            loop(BACK, GROUP, lambda s: finish(h, s, True))

        def add(s, carry):
            top, bottom = carry
            at = pl.multiple_of(s * ROWS, ROWS)
            lat = lbuf[s]
            top = top + first_first(lat, stg[3, h, pl.ds(at, 128)])
            bottom = bottom + first_first(lat, stg[3, h, pl.ds(at + 128, 128)])
            return top, bottom

        zeros = jnp.zeros((128, 128), F32)
        top, bottom = lax.fori_loop(0, GROUP, add, (zeros, zeros))
        dwp[h] = top[0:64] + bottom[64:128]

        def send(j):
            @pl.when(rs_self(h, j))
            def _():
                local(dwp.at[h, pl.ds(pl.multiple_of(8 * j, 8), 8)],
                      rsb.at[h, dp * 2 + xhi], rs_r.at[h]).start()

            @pl.when(jnp.logical_not(rs_self(h, j)))
            def _():
                rs_copy(h, j).start()

        loop(0, 8, send)

    def head(h):
        for a, (_, buf, off) in enumerate(arrays):
            await_bytes(buf.at[h, pl.ds(off, OWN)], in_r.at[h, a])

        def add_latents(s):
            lat = lbuf[s]
            at = pl.multiple_of(HALO + s * ROWS, ROWS)
            cols = pl.ds(pl.multiple_of(h * DH, DH), DH)
            upper = pl.ds(at, 128)
            lower = pl.ds(at + 128, 128)
            vb[h, upper] = (vb[h, upper].astype(F32) + dot(lat, w2[64:192, cols])).astype(BF16)
            vb[h, lower] = (vb[h, lower].astype(F32) + dot(lat, w2[0:128, cols])).astype(BF16)

        @pl.when(first)
        def _():
            halo_copy(h, 0).start()

        loop(0, GROUP, add_latents)

        @pl.when(first)
        def _():
            halo_copy(h, 1).start()

        acc_k[h] = jnp.zeros((HALO + OWN, DH), F32)
        acc_v[h] = jnp.zeros((HALO + OWN, DH), F32)

        loop(BACK, GROUP, lambda i: stretch(h, i))

        @pl.when(jnp.logical_not(first))
        def _():
            await_bytes(kb.at[h, pl.ds(0, HALO)], halo_r.at[h, 0])
            await_bytes(vb.at[h, pl.ds(0, HALO)], halo_r.at[h, 1])

        loop(0, BACK, lambda i: stretch(h, i))

        @pl.when(jnp.logical_not(first))
        def _():
            part_out[h, 0] = (acc_k[h, 0:HALO] * SCALE).astype(BF16)
            part_out[h, 1] = acc_v[h, 0:HALO].astype(BF16)
            part_copy(h).start()

        loop(0, BACK, lambda s: finish(h, s, False))

        @pl.when(jnp.logical_not(first))
        def _():
            loop(BACK, GROUP, lambda s: finish(h, s, False))

        @pl.when(h > 0)
        def _():
            late(h - 1)

    loop(0, HEADS, head)

    def ag_copy(h, n):
        return remote(agb.at[h, g], agb.at[h, g], ag_s.at[h], ag_r.at[h], group_dev(peer(n)))

    def add_up(h):
        @pl.when(xhi == owner_of(h))
        def _():
            await_bytes(rsb.at[h], rs_r.at[h])
            agb[h, g] = jnp.sum(rsb[h], axis=0)
            loop(1, GROUP, lambda n: ag_copy(h, n).start())

    def spread(h):
        @pl.when(xhi == owner_of(h))
        def _():
            await_bytes(agb.at[h, 0:GROUP - 1], ag_r.at[h])
            local(agb.at[h], plb.at[h * 8 + dp], pl_r.at[h]).start()
            loop(1, 16, lambda n: remote(
                agb.at[h], plb.at[h * 8 + dp], pl_s.at[h], pl_r.at[h], plane_dev(n)).start())

    add_up(0)
    late(2)
    add_up(1)
    add_up(2)
    loop(0, GROUP, lambda s: send_sums(HEADS - 1, s))
    loop(0, HEADS, spread)

    def assemble(h):
        await_bytes(plb.at[pl.ds(h * 8, 8)], pl_r.at[h])
        for j in range(8):
            for p in range(GROUP):
                dw_ref[8 * j:8 * j + 8, (HEADS * p + h) * DH:(HEADS * p + h + 1) * DH] = (
                    plb[h * 8 + j, p])

    for h in range(HEADS):
        assemble(h)

    for a, ref in enumerate((out_ref, dq_ref, dk_ref, dv_ref)):
        await_bytes(ref, fin_r.at[a])

    def wait_main(c):
        @pl.when(jnp.logical_not(is_self(c, self_main)))
        def _():
            main_copy(c).wait_send()

    def wait_carry(c):
        @pl.when(jnp.logical_not(is_self(c, self_carry)))
        def _():
            carry_copy(c).wait_send()

    loop(0, 8, wait_main)

    @pl.when(last_slab)
    def _():
        loop(0, 8, wait_carry)

    await_bytes(vbuf.at[0:GROUP - 1], val_s.at[0])
    await_bytes(lbuf.at[0:GROUP - 1], lat_s.at[0])

    @pl.when(first)
    def _():
        await_bytes(vbuf.at[0:BACK], val_s.at[1])

    def drain(h):
        for a in range(4):
            await_bytes(qb.at[h, pl.ds(0, OWN - ROWS)], in_s.at[h, a])
            await_bytes(stg.at[a, h, pl.ds(0, OWN - ROWS)], fin_s.at[h, a])

        @pl.when(first)
        def _():
            await_bytes(kb.at[h, pl.ds(0, HALO)], halo_s.at[h, 0])
            await_bytes(vb.at[h, pl.ds(0, HALO)], halo_s.at[h, 1])

        @pl.when(jnp.logical_not(first))
        def _():
            await_bytes(part_out.at[h], part_s.at[h])

        def wait_rs(j):
            @pl.when(jnp.logical_not(rs_self(h, j)))
            def _():
                rs_copy(h, j).wait_send()

        loop(0, 8, wait_rs)

        @pl.when(xhi == owner_of(h))
        def _():
            await_bytes(agb.at[h, 0:GROUP - 1], ag_s.at[h])
            await_bytes(plb.at[0:15], pl_s.at[h])

    loop(0, HEADS, drain)


def settle(*refs):
    srcs, dsts, bufs, (sems_in, sems_out) = refs[0:5], refs[5:10], refs[10:15], refs[15:17]
    pieces = []
    for src, dst, buf in zip(srcs, dsts, bufs):
        half = src.shape[0] // 2
        for at in (0, half):
            cut = pl.ds(at, half)
            n = len(pieces)
            pieces.append((
                pltpu.make_async_copy(src.at[cut], buf.at[cut], sems_in.at[n]),
                pltpu.make_async_copy(buf.at[cut], dst.at[cut], sems_out.at[n])))
    for into, _ in pieces:
        into.start()
    for into, outof in pieces:
        into.wait()
        outof.start()
    for _, outof in pieces:
        outof.wait()


def on_device(enc_feat, conv_w, w_lat, q_raw, k_raw, v_in, valid, d_out):
    feat = enc_feat.reshape(ROWS, enc_feat.shape[3])
    taps = conv_w.swapaxes(1, 2).reshape(-1, conv_w.shape[1])
    result = jax.ShapeDtypeStruct((ROWS, q_raw.shape[2]), BF16)
    anywhere = pl.BlockSpec(memory_space=pl.ANY)
    vmem = pl.BlockSpec(memory_space=pltpu.VMEM)
    dma = pltpu.SemaphoreType.DMA
    results = pl.pallas_call(
        kernel,
        out_shape=(result, result, result, result,
                   jax.ShapeDtypeStruct(w_lat.shape, F32)),
        in_specs=[pl.BlockSpec(memory_space=pltpu.SMEM), vmem, vmem] + [anywhere] * 5,
        out_specs=(anywhere,) * 4 + (vmem,),
        scratch_shapes=[
            pltpu.VMEM((HEADS, OWN, DH), BF16),
            pltpu.VMEM((HEADS, OWN, DH), BF16),
            pltpu.VMEM((HEADS, HALO + OWN, DH), BF16),
            pltpu.VMEM((HEADS, HALO + OWN, DH), BF16),
            pltpu.VMEM((HEADS, HALO + OWN, DH), F32),
            pltpu.VMEM((HEADS, HALO + OWN, DH), F32),
            pltpu.VMEM((4, HEADS, OWN, DH), BF16),
            pltpu.VMEM((HEADS, 2, HALO, DH), BF16),
            pltpu.VMEM((HEADS, 2, HALO, DH), BF16),
            pltpu.VMEM((HALO + OWN, ROWS), F32),
            pltpu.VMEM((BACK + GROUP, 8, 128), jnp.int32),
            pltpu.VMEM((8, 128), jnp.int32),
            pltpu.VMEM((192, HEADS * DH), BF16),
            pltpu.VMEM((GROUP, 128, 128), BF16),
            pltpu.VMEM((8, 32, 128), F32),
            pltpu.VMEM((9, 32, 128), F32),
            pltpu.VMEM((HEADS, 64, 128), F32),
            pltpu.VMEM((HEADS, 16, 8, 128), F32),
            pltpu.VMEM((HEADS, GROUP, 8, 128), F32),
            pltpu.VMEM((HEADS * 8, GROUP, 8, 128), F32),
            dma((HEADS, 4)), dma((HEADS, 4)),
            dma((HEADS, 4)), dma((4,)),
            dma((HEADS, 2)), dma((HEADS, 2)),
            dma((HEADS,)), dma((HEADS,)),
            dma((2,)), dma((2,)),
            dma((1,)), dma((1,)),
            dma((2, 8)), dma((1,)),
            dma((HEADS, 8)), dma((HEADS,)),
            dma((HEADS,)), dma((HEADS,)),
            dma((HEADS,)), dma((HEADS,)),
            dma((1,)),
        ],
        name="slab_attention",
        compiler_params=pltpu.CompilerParams(
            collective_id=0, has_side_effects=True, vmem_limit_bytes=60 * 1024 * 1024),
    )(valid, feat, taps, w_lat, q_raw[0], k_raw[0], v_in[0], d_out[0])
    out, dq, dk, dv, dw = pl.pallas_call(
        settle,
        out_shape=tuple(jax.ShapeDtypeStruct(r.shape, r.dtype) for r in results),
        in_specs=[anywhere] * 5,
        out_specs=(anywhere,) * 5,
        scratch_shapes=[pltpu.VMEM(r.shape, r.dtype) for r in results] + [dma((10,)), dma((10,))],
        name="settle",
        compiler_params=pltpu.CompilerParams(vmem_limit_bytes=60 * 1024 * 1024),
    )(*results)
    return out[None], dq[None], dk[None], dv[None], dw


def solution(mesh):
    tokens = P("dp", "ctx", None)
    return jax.shard_map(
        on_device,
        mesh=mesh,
        in_specs=(P(None, ("dp", "ctx"), None, None), P(), P(), tokens, tokens, tokens,
                  P("dp", "ctx"), tokens),
        out_specs=(tokens, tokens, tokens, tokens, P()),
        check_vma=False,
    )
```

```python
import math

import jax
import jax.numpy as jnp
from jax import lax
from jax.experimental import pallas as pl
from jax.experimental.pallas import tpu as pltpu
from jax.sharding import PartitionSpec as P

MESH = pl.DeviceIdType.MESH
DH = 128
ROWS = 256
GROUP = 8
HEADS = 3
BACK = 4
HALO = BACK * ROWS
OWN = GROUP * ROWS
SPAN = (BACK + 1) * ROWS
SCALE = 1.0 / math.sqrt(DH)
EXP2 = SCALE * math.log2(math.e)
MASKED = -1e30
F32 = jnp.float32
BF16 = jnp.bfloat16


def last_last(a, b):
    return lax.dot_general(a, b, (((1,), (1,)), ((), ())), preferred_element_type=F32)


def first_first(a, b):
    return lax.dot_general(a, b, (((0,), (0,)), ((), ())), preferred_element_type=F32)


def dot(a, b):
    return jnp.dot(a, b, preferred_element_type=F32)


def kernel(
    count_ref, feat_ref, taps_ref, wlat_ref, q_ref, k_ref, v_ref, do_ref,
    out_ref, dq_ref, dk_ref, dv_ref, dw_ref,
    qb, dob, kb, vb, acc_k, acc_v, stg, part_out, part_in, bias, vbuf, valid_ref, w2, lbuf,
    pk_out, pk_in, dwp, rsb, agb, plb,
    in_s, in_r, fin_s, fin_r, halo_s, halo_r, part_s, part_r, val_s, val_r,
    lat_s, lat_r, enc_s, enc_r, rs_s, rs_r, ag_s, ag_r, pl_s, pl_r, loc,
):
    dp = lax.axis_index("dp")
    ctx = lax.axis_index("ctx")
    xhi = ctx // GROUP
    g = ctx % GROUP
    first = xhi == 0
    partner = (dp, ctx + GROUP - 2 * GROUP * xhi)
    slab_stretch = dp * 2 + xhi
    next_stretch = (slab_stretch + 1) % 16
    self_main = ctx == slab_stretch
    self_carry = ctx == next_stretch
    last_slab = g == GROUP - 1

    def remote(src, dst, ss, rs, dev):
        return pltpu.make_async_remote_copy(
            src_ref=src, dst_ref=dst, send_sem=ss, recv_sem=rs, device_id=dev,
            device_id_type=MESH)

    def local(src, dst, sem):
        return pltpu.make_async_copy(src, dst, sem)

    def await_bytes(ref, sem):
        pltpu.make_async_copy(ref, ref, sem).wait()

    def peer(n):
        return (g + n) % GROUP

    def group_dev(p):
        return (dp, xhi * GROUP + p)

    def loop(lo, hi, body):
        lax.fori_loop(lo, hi, lambda i, c: (body(i), c)[1], 0)

    barrier = pltpu.get_barrier_semaphore()

    def signal(dev):
        pl.semaphore_signal(barrier, inc=1, device_id=dev, device_id_type=MESH)

    loop(1, GROUP, lambda n: signal(group_dev(peer(n))))

    def plane_dev(n):
        m = (dp * 2 + xhi + n) % 16
        return (m // 2, (m % 2) * GROUP + g)

    loop(1, 16, lambda n: signal(plane_dev(n)))
    src_dp = ctx // 2
    src_ctx = (ctx % 2) * GROUP

    def signal_source(i):
        @pl.when(jnp.logical_or(src_dp != dp, src_ctx + i != ctx))
        def _():
            signal((src_dp, src_ctx + i))

    loop(0, GROUP, signal_source)
    prev = (ctx + 15) % 16
    prev_dp = prev // 2
    prev_ctx = (prev % 2) * GROUP + GROUP - 1

    @pl.when(jnp.logical_or(prev_dp != dp, prev_ctx != ctx))
    def _():
        signal((prev_dp, prev_ctx))

    one = jnp.int32(1)
    zero = jnp.int32(0)
    expected = (
        (GROUP - 1) + 15 + 8 - jnp.where(self_main, one, zero)
        + jnp.where(last_slab, 8 - jnp.where(self_carry, one, zero), zero)
    )

    local(wlat_ref.at[:, pl.ds(pl.multiple_of(g * HEADS * DH, DH), HEADS * DH)],
          w2.at[pl.ds(64, 64)], loc.at[0]).start()
    valid_ref[...] = jnp.full((8, 128), count_ref[0, 0], jnp.int32)
    a4 = last_last(feat_ref[...], taps_ref[0:128]).reshape(8, 2, 16, 128)
    b4 = last_last(feat_ref[...], taps_ref[64:192]).reshape(8, 2, 16, 128)
    mix = a4[:, 1] + b4[:, 0]
    low = lax.broadcasted_iota(jnp.int32, (8, 16, 128), 2) < 64
    pk_out[:, 0:16, :] = jnp.where(low, a4[:, 0], mix)
    pk_out[:, 16:32, :] = jnp.where(low, mix, b4[:, 1])

    pl.semaphore_wait(barrier, expected)

    def main_copy(c):
        return remote(pk_out.at[c], pk_in.at[1 + g], enc_s.at[0, c], enc_r.at[0],
                      (c, slab_stretch))

    def carry_copy(c):
        return remote(pk_out.at[c], pk_in.at[0], enc_s.at[1, c], enc_r.at[0],
                      (c, next_stretch))

    def is_self(c, own):
        return jnp.logical_and(own, c == dp)

    def send_main(c):
        @pl.when(is_self(c, self_main))
        def _():
            local(pk_out.at[c], pk_in.at[1 + g], enc_r.at[0]).start()

        @pl.when(jnp.logical_not(is_self(c, self_main)))
        def _():
            main_copy(c).start()

    def send_carry(c):
        @pl.when(is_self(c, self_carry))
        def _():
            local(pk_out.at[c], pk_in.at[0], enc_r.at[0]).start()

        @pl.when(jnp.logical_not(is_self(c, self_carry)))
        def _():
            carry_copy(c).start()

    loop(0, 8, send_main)

    @pl.when(last_slab)
    def _():
        loop(0, 8, send_carry)

    local(valid_ref, vbuf.at[BACK + g], val_r.at[0]).start()
    loop(1, GROUP, lambda n: remote(
        valid_ref, vbuf.at[BACK + g], val_s.at[0], val_r.at[0],
        group_dev(peer(n))).start())

    arrays = ((k_ref, kb, HALO), (q_ref, qb, 0), (do_ref, dob, 0), (v_ref, vb, HALO))

    def send_head(h):
        for a, (src, buf, off) in enumerate(arrays):
            dst = buf.at[h, pl.ds(pl.multiple_of(off + g * ROWS, ROWS), ROWS)]

            def cols(p):
                return src.at[:, pl.ds(pl.multiple_of((HEADS * p + h) * DH, DH), DH)]

            local(cols(g), dst, in_r.at[h, a]).start()
            loop(1, GROUP, lambda n: remote(
                cols(peer(n)), dst, in_s.at[h, a], in_r.at[h, a],
                group_dev(peer(n))).start())

    send_head(0)

    w2[0:64, :] = jnp.zeros((64, HEADS * DH), BF16)
    w2[128:192, :] = jnp.zeros((64, HEADS * DH), BF16)

    @pl.when(first)
    def _():
        kb[:, 0:HALO, :] = jnp.zeros((HEADS, HALO, DH), BF16)
        vb[:, 0:HALO, :] = jnp.zeros((HEADS, HALO, DH), BF16)
        vbuf[0:BACK] = jnp.zeros((BACK, 8, 128), jnp.int32)
        lbuf[0:BACK] = jnp.zeros((BACK, 128, 128), BF16)

    await_bytes(pk_in, enc_r.at[0])
    before = jnp.concatenate(
        [jnp.where(ctx == 0, jnp.zeros((1, 32, 128), F32), pk_in[0:1]), pk_in[1:8]], axis=0)
    x = (pk_in[1:9] + pltpu.roll(before, 64, 2)).reshape(ROWS, 128)
    lat_low = lax.broadcasted_iota(jnp.int32, (128, 128), 1) < 64
    lbuf[BACK + g] = jnp.where(lat_low, x[0:128], pltpu.roll(x[128:256], 64, 1)).astype(BF16)
    loop(1, GROUP, lambda n: remote(
        lbuf.at[BACK + g], lbuf.at[BACK + g], lat_s.at[0], lat_r.at[0], group_dev(peer(n))).start())

    send_head(1)
    send_head(2)

    await_bytes(vbuf.at[BACK:], val_r.at[0])
    halo_valid = remote(vbuf.at[pl.ds(GROUP, BACK)], vbuf.at[pl.ds(0, BACK)],
                        val_s.at[1], val_r.at[1], partner)

    @pl.when(first)
    def _():
        halo_valid.start()

    @pl.when(jnp.logical_not(first))
    def _():
        await_bytes(vbuf.at[0:BACK], val_r.at[1])

    def make_bias(s):
        rows = lax.broadcasted_iota(jnp.int32, (ROWS, 128), 0)
        ok = rows < vbuf[s, 0:1, :]
        col = jnp.where(ok, jnp.zeros((ROWS, 128), F32), jnp.full((ROWS, 128), MASKED, F32))
        at = pl.ds(pl.multiple_of(s * ROWS, ROWS), ROWS)
        bias[at, 0:128] = col
        bias[at, 128:256] = col

    loop(0, BACK + GROUP, make_bias)
    local(wlat_ref.at[:, pl.ds(0, HEADS * DH)], w2.at[pl.ds(64, 64)], loc.at[0]).wait()
    await_bytes(lbuf.at[0:GROUP - 1], lat_r.at[0])
    halo_latents = remote(lbuf.at[pl.ds(GROUP, BACK)], lbuf.at[pl.ds(0, BACK)],
                          lat_s.at[1], lat_r.at[1], partner)

    @pl.when(first)
    def _():
        halo_latents.start()

    @pl.when(jnp.logical_not(first))
    def _():
        await_bytes(lbuf.at[0:BACK], lat_r.at[1])

    def halo_copy(h, a):
        buf = (kb, vb)[a]
        return remote(buf.at[h, pl.ds(OWN, HALO)], buf.at[h, pl.ds(0, HALO)],
                      halo_s.at[h, a], halo_r.at[h, a], partner)

    def part_copy(h):
        return remote(part_out.at[h], part_in.at[h], part_s.at[h], part_r.at[h], partner)

    def send_result(h, a, s):
        ref = (out_ref, dq_ref, dk_ref, dv_ref)[a]
        src = stg.at[a, h, pl.ds(pl.multiple_of(s * ROWS, ROWS), ROWS)]
        dst = ref.at[:, pl.ds(pl.multiple_of((HEADS * g + h) * DH, DH), DH)]

        @pl.when(s == g)
        def _():
            local(src, dst, fin_r.at[a]).start()

        @pl.when(s != g)
        def _():
            remote(src, dst, fin_s.at[h, a], fin_r.at[a], group_dev(s)).start()

    def stretch(h, i):
        rows = pl.ds(pl.multiple_of(i * ROWS, ROWS), ROWS)
        span = pl.ds(pl.multiple_of(i * ROWS, ROWS), SPAN)
        q = qb[h, rows]
        do = dob[h, rows]
        keys = kb[h, span]
        vals = vb[h, span]
        s = last_last(keys, q) + bias[span, :]
        m = jnp.max(s, axis=0, keepdims=True)
        e = jnp.exp2((s - m) * EXP2)
        p = e * (1.0 / jnp.sum(e, axis=0, keepdims=True))
        p_low = p.astype(BF16)
        out_t = first_first(vals, p_low)
        out = out_t.T.astype(BF16)
        stg[0, h, rows] = out
        delta = jnp.sum(do.astype(F32).T * out_t.astype(BF16).astype(F32), axis=0, keepdims=True)
        grad = last_last(vals, do)
        ds = (p * (grad - delta)).astype(BF16)
        stg[1, h, rows] = (first_first(keys, ds) * SCALE).T.astype(BF16)
        acc_k[h, span] += dot(ds, q)
        acc_v[h, span] += dot(p_low, do)
        send_result(h, 0, i)
        send_result(h, 1, i)

    def finish(h, s, with_part):
        rows = pl.ds(pl.multiple_of(HALO + s * ROWS, ROWS), ROWS)
        dk = acc_k[h, rows] * SCALE
        dv = acc_v[h, rows]
        if with_part:
            at = pl.ds(pl.multiple_of((s - BACK) * ROWS, ROWS), ROWS)
            dk = dk + part_in[h, 0, at].astype(F32)
            dv = dv + part_in[h, 1, at].astype(F32)
        own = pl.ds(pl.multiple_of(s * ROWS, ROWS), ROWS)
        stg[2, h, own] = dk.astype(BF16)
        stg[3, h, own] = dv.astype(BF16)

        send_result(h, 2, s)
        send_result(h, 3, s)

    def owner_of(h, j):
        return (h + j) % 2

    def owns(h):
        return xhi == owner_of(h, dp)

    def rs_copy(h, j):
        return remote(
            dwp.at[h, pl.ds(pl.multiple_of(8 * j, 8), 8)], rsb.at[h, dp * 2 + xhi],
            rs_s.at[h, j], rs_r.at[h], (j, owner_of(h, j) * GROUP + g))

    def rs_self(h, j):
        return jnp.logical_and(j == dp, owns(h))

    def own_sums(h):
        loop(0, BACK, lambda s: finish(h, s, False))

        @pl.when(jnp.logical_not(first))
        def _():
            loop(BACK, GROUP, lambda s: finish(h, s, False))

    def late_sums(h):
        @pl.when(first)
        def _():
            await_bytes(part_in.at[h], part_r.at[h])
            loop(BACK, GROUP, lambda s: finish(h, s, True))

    def share(h):
        def add(s, carry):
            top, bottom = carry
            at = pl.multiple_of(s * ROWS, ROWS)
            lat = lbuf[s]
            top = top + first_first(lat, acc_v[h, pl.ds(at, 128)].astype(BF16))
            bottom = bottom + first_first(lat, acc_v[h, pl.ds(at + 128, 128)].astype(BF16))
            return top, bottom

        zeros = jnp.zeros((128, 128), F32)
        top, bottom = lax.fori_loop(0, BACK + GROUP, add, (zeros, zeros))
        dwp[h] = top[0:64] + bottom[64:128]

        def send(j):
            @pl.when(rs_self(h, j))
            def _():
                local(dwp.at[h, pl.ds(pl.multiple_of(8 * j, 8), 8)],
                      rsb.at[h, dp * 2 + xhi], rs_r.at[h]).start()

            @pl.when(jnp.logical_not(rs_self(h, j)))
            def _():
                rs_copy(h, j).start()

        loop(0, 8, send)

    def ag_copy(h, n):
        return remote(agb.at[h, g], agb.at[h, g], ag_s.at[h], ag_r.at[h], group_dev(peer(n)))

    def add_up(h):
        @pl.when(owns(h))
        def _():
            await_bytes(rsb.at[h], rs_r.at[h])
            agb[h, g] = jnp.sum(rsb[h], axis=0)
            loop(1, GROUP, lambda n: ag_copy(h, n).start())

    def spread(h):
        @pl.when(owns(h))
        def _():
            await_bytes(agb.at[h, 0:GROUP - 1], ag_r.at[h])
            local(agb.at[h], plb.at[h * 8 + dp], pl_r.at[h]).start()
            loop(1, 16, lambda n: remote(
                agb.at[h], plb.at[h * 8 + dp], pl_s.at[h], pl_r.at[h], plane_dev(n)).start())

    def head(h):
        @pl.when(h == 2)
        def _():
            add_up(0)

        for a, (_, buf, off) in enumerate(arrays):
            await_bytes(buf.at[h, pl.ds(off, OWN)], in_r.at[h, a])

        def add_latents(s):
            lat = lbuf[BACK + s]
            at = pl.multiple_of(HALO + s * ROWS, ROWS)
            cols = pl.ds(pl.multiple_of(h * DH, DH), DH)
            upper = pl.ds(at, 128)
            lower = pl.ds(at + 128, 128)
            vb[h, upper] = (vb[h, upper].astype(F32) + dot(lat, w2[64:192, cols])).astype(BF16)
            vb[h, lower] = (vb[h, lower].astype(F32) + dot(lat, w2[0:128, cols])).astype(BF16)

        @pl.when(first)
        def _():
            halo_copy(h, 0).start()

        loop(0, GROUP, add_latents)

        @pl.when(first)
        def _():
            halo_copy(h, 1).start()

        acc_k[h] = jnp.zeros((HALO + OWN, DH), F32)
        acc_v[h] = jnp.zeros((HALO + OWN, DH), F32)

        loop(BACK, GROUP, lambda i: stretch(h, i))

        @pl.when(jnp.logical_not(first))
        def _():
            await_bytes(kb.at[h, pl.ds(0, HALO)], halo_r.at[h, 0])
            await_bytes(vb.at[h, pl.ds(0, HALO)], halo_r.at[h, 1])

        loop(0, BACK, lambda i: stretch(h, i))

        @pl.when(jnp.logical_not(first))
        def _():
            part_out[h, 0] = (acc_k[h, 0:HALO] * SCALE).astype(BF16)
            part_out[h, 1] = acc_v[h, 0:HALO].astype(BF16)
            part_copy(h).start()

        share(h)

        @pl.when(h == 0)
        def _():
            own_sums(0)

        @pl.when(h == 1)
        def _():
            late_sums(0)

    loop(0, HEADS, head)

    add_up(1)
    spread(0)
    add_up(2)
    own_sums(1)
    late_sums(1)
    own_sums(2)
    spread(1)
    spread(2)
    late_sums(2)

    def assemble(h):
        await_bytes(plb.at[pl.ds(h * 8, 8)], pl_r.at[h])
        for j in range(8):
            for p in range(GROUP):
                dw_ref[8 * j:8 * j + 8, (HEADS * p + h) * DH:(HEADS * p + h + 1) * DH] = (
                    plb[h * 8 + j, p])

    for h in range(HEADS):
        assemble(h)

    for a, ref in enumerate((out_ref, dq_ref, dk_ref, dv_ref)):
        await_bytes(ref, fin_r.at[a])

    def wait_main(c):
        @pl.when(jnp.logical_not(is_self(c, self_main)))
        def _():
            main_copy(c).wait_send()

    def wait_carry(c):
        @pl.when(jnp.logical_not(is_self(c, self_carry)))
        def _():
            carry_copy(c).wait_send()

    loop(0, 8, wait_main)

    @pl.when(last_slab)
    def _():
        loop(0, 8, wait_carry)

    await_bytes(vbuf.at[0:GROUP - 1], val_s.at[0])
    await_bytes(lbuf.at[0:GROUP - 1], lat_s.at[0])

    @pl.when(first)
    def _():
        await_bytes(vbuf.at[0:BACK], val_s.at[1])
        await_bytes(lbuf.at[0:BACK], lat_s.at[1])

    def drain(h):
        for a in range(4):
            await_bytes(qb.at[h, pl.ds(0, OWN - ROWS)], in_s.at[h, a])
            await_bytes(stg.at[a, h, pl.ds(0, OWN - ROWS)], fin_s.at[h, a])

        @pl.when(first)
        def _():
            await_bytes(kb.at[h, pl.ds(0, HALO)], halo_s.at[h, 0])
            await_bytes(vb.at[h, pl.ds(0, HALO)], halo_s.at[h, 1])

        @pl.when(jnp.logical_not(first))
        def _():
            await_bytes(part_out.at[h], part_s.at[h])

        def wait_rs(j):
            @pl.when(jnp.logical_not(rs_self(h, j)))
            def _():
                rs_copy(h, j).wait_send()

        loop(0, 8, wait_rs)

        @pl.when(owns(h))
        def _():
            await_bytes(agb.at[h, 0:GROUP - 1], ag_s.at[h])
            await_bytes(plb.at[0:15], pl_s.at[h])

    loop(0, HEADS, drain)


def settle(*refs):
    srcs, dsts, sem = refs[0:5], refs[5:10], refs[10]
    copies = [pltpu.make_async_copy(src, dst, sem.at[n])
              for n, (src, dst) in enumerate(zip(srcs, dsts))]
    for copy in copies:
        copy.start()
    for copy in copies:
        copy.wait()


def on_device(enc_feat, conv_w, w_lat, q_raw, k_raw, v_in, valid, d_out):
    feat = enc_feat.reshape(ROWS, enc_feat.shape[3])
    taps = conv_w.swapaxes(1, 2).reshape(-1, conv_w.shape[1])
    result = pltpu.VMEM((ROWS, q_raw.shape[2]), BF16)
    anywhere = pl.BlockSpec(memory_space=pl.ANY)
    vmem = pl.BlockSpec(memory_space=pltpu.VMEM)
    dma = pltpu.SemaphoreType.DMA
    results = pl.pallas_call(
        kernel,
        out_shape=(result, result, result, result,
                   pltpu.VMEM(w_lat.shape, F32)),
        in_specs=[pl.BlockSpec(memory_space=pltpu.SMEM), vmem, vmem] + [anywhere] * 5,
        out_specs=(vmem,) * 5,
        scratch_shapes=[
            pltpu.VMEM((HEADS, OWN, DH), BF16),
            pltpu.VMEM((HEADS, OWN, DH), BF16),
            pltpu.VMEM((HEADS, HALO + OWN, DH), BF16),
            pltpu.VMEM((HEADS, HALO + OWN, DH), BF16),
            pltpu.VMEM((HEADS, HALO + OWN, DH), F32),
            pltpu.VMEM((HEADS, HALO + OWN, DH), F32),
            pltpu.VMEM((4, HEADS, OWN, DH), BF16),
            pltpu.VMEM((HEADS, 2, HALO, DH), BF16),
            pltpu.VMEM((HEADS, 2, HALO, DH), BF16),
            pltpu.VMEM((HALO + OWN, ROWS), F32),
            pltpu.VMEM((BACK + GROUP, 8, 128), jnp.int32),
            pltpu.VMEM((8, 128), jnp.int32),
            pltpu.VMEM((192, HEADS * DH), BF16),
            pltpu.VMEM((BACK + GROUP, 128, 128), BF16),
            pltpu.VMEM((8, 32, 128), F32),
            pltpu.VMEM((9, 32, 128), F32),
            pltpu.VMEM((HEADS, 64, 128), F32),
            pltpu.VMEM((HEADS, 16, 8, 128), F32),
            pltpu.VMEM((HEADS, GROUP, 8, 128), F32),
            pltpu.VMEM((HEADS * 8, GROUP, 8, 128), F32),
            dma((HEADS, 4)), dma((HEADS, 4)),
            dma((HEADS, 4)), dma((4,)),
            dma((HEADS, 2)), dma((HEADS, 2)),
            dma((HEADS,)), dma((HEADS,)),
            dma((2,)), dma((2,)),
            dma((2,)), dma((2,)),
            dma((2, 8)), dma((1,)),
            dma((HEADS, 8)), dma((HEADS,)),
            dma((HEADS,)), dma((HEADS,)),
            dma((HEADS,)), dma((HEADS,)),
            dma((1,)),
        ],
        name="slab_attention",
        compiler_params=pltpu.CompilerParams(
            collective_id=0, has_side_effects=True, vmem_limit_bytes=57 * 1024 * 1024),
    )(valid, feat, taps, w_lat, q_raw[0], k_raw[0], v_in[0], d_out[0])
    out, dq, dk, dv, dw = pl.pallas_call(
        settle,
        out_shape=tuple(jax.ShapeDtypeStruct(r.shape, r.dtype) for r in results),
        in_specs=[vmem] * 5,
        out_specs=(anywhere,) * 5,
        scratch_shapes=[dma((5,))],
        name="settle",
        compiler_params=pltpu.CompilerParams(vmem_limit_bytes=16 * 1024 * 1024),
    )(*(pltpu.with_memory_space_constraint(r, pltpu.VMEM) for r in results))
    return out[None], dq[None], dk[None], dv[None], dw


def solution(mesh):
    tokens = P("dp", "ctx", None)
    return jax.shard_map(
        on_device,
        mesh=mesh,
        in_specs=(P(None, ("dp", "ctx"), None, None), P(), P(), tokens, tokens, tokens,
                  P("dp", "ctx"), tokens),
        out_specs=(tokens, tokens, tokens, tokens, P()),
        check_vma=False,
    )
```

```python
import math

import jax
import jax.numpy as jnp
from jax import lax
from jax.experimental import pallas as pl
from jax.experimental.pallas import tpu as pltpu
from jax.sharding import PartitionSpec as P

MESH = pl.DeviceIdType.MESH
DH = 128
ROWS = 256
GROUP = 8
HEADS = 3
BACK = 4
HALO = BACK * ROWS
OWN = GROUP * ROWS
SPAN = (BACK + 1) * ROWS
SCALE = 1.0 / math.sqrt(DH)
EXP2 = SCALE * math.log2(math.e)
MASKED = -1e30
F32 = jnp.float32
BF16 = jnp.bfloat16


def last_last(a, b):
    return lax.dot_general(a, b, (((1,), (1,)), ((), ())), preferred_element_type=F32)


def first_first(a, b):
    return lax.dot_general(a, b, (((0,), (0,)), ((), ())), preferred_element_type=F32)


def dot(a, b):
    return jnp.dot(a, b, preferred_element_type=F32)


def kernel(
    count_ref, feat_ref, taps_ref, wlat_ref, q_ref, k_ref, v_ref, do_ref,
    out_ref, dq_ref, dk_ref, dv_ref, dw_ref,
    qb, dob, kb, vb, acc_k, acc_v, stg, part_out, part_in, bias, vbuf, valid_ref, w2, lbuf,
    pk_out, pk_in, dwp, rsb, agb, plb,
    in_s, in_r, fin_s, fin_r, halo_s, halo_r, part_s, part_r, val_s, val_r,
    lat_s, lat_r, enc_s, enc_r, rs_s, rs_r, ag_s, ag_r, pl_s, pl_r, loc,
):
    dp = lax.axis_index("dp")
    ctx = lax.axis_index("ctx")
    xhi = ctx // GROUP
    g = ctx % GROUP
    first = xhi == 0
    partner = (dp, ctx + GROUP - 2 * GROUP * xhi)
    slab_stretch = dp * 2 + xhi
    next_stretch = (slab_stretch + 1) % 16
    self_main = ctx == slab_stretch
    self_carry = ctx == next_stretch
    last_slab = g == GROUP - 1

    def remote(src, dst, ss, rs, dev):
        return pltpu.make_async_remote_copy(
            src_ref=src, dst_ref=dst, send_sem=ss, recv_sem=rs, device_id=dev,
            device_id_type=MESH)

    def local(src, dst, sem):
        return pltpu.make_async_copy(src, dst, sem)

    def await_bytes(ref, sem):
        pltpu.make_async_copy(ref, ref, sem).wait()

    def peer(n):
        return (g + n) % GROUP

    def group_dev(p):
        return (dp, xhi * GROUP + p)

    def loop(lo, hi, body):
        lax.fori_loop(lo, hi, lambda i, c: (body(i), c)[1], 0)

    barrier = pltpu.get_barrier_semaphore()

    def signal(dev):
        pl.semaphore_signal(barrier, inc=1, device_id=dev, device_id_type=MESH)

    loop(1, GROUP, lambda n: signal(group_dev(peer(n))))

    def plane_dev(n):
        m = (dp * 2 + xhi + n) % 16
        return (m // 2, (m % 2) * GROUP + g)

    loop(1, 16, lambda n: signal(plane_dev(n)))
    src_dp = ctx // 2
    src_ctx = (ctx % 2) * GROUP

    def signal_source(i):
        @pl.when(jnp.logical_or(src_dp != dp, src_ctx + i != ctx))
        def _():
            signal((src_dp, src_ctx + i))

    loop(0, GROUP, signal_source)
    prev = (ctx + 15) % 16
    prev_dp = prev // 2
    prev_ctx = (prev % 2) * GROUP + GROUP - 1

    @pl.when(jnp.logical_or(prev_dp != dp, prev_ctx != ctx))
    def _():
        signal((prev_dp, prev_ctx))

    one = jnp.int32(1)
    zero = jnp.int32(0)
    expected = (
        (GROUP - 1) + 15 + 8 - jnp.where(self_main, one, zero)
        + jnp.where(last_slab, 8 - jnp.where(self_carry, one, zero), zero)
    )

    local(wlat_ref.at[:, pl.ds(pl.multiple_of(g * HEADS * DH, DH), HEADS * DH)],
          w2.at[pl.ds(64, 64)], loc.at[0]).start()
    valid_ref[...] = jnp.broadcast_to(count_ref[...], (8, 128))
    a4 = last_last(feat_ref[...], taps_ref[0:128]).reshape(8, 2, 16, 128)
    b4 = last_last(feat_ref[...], taps_ref[64:192]).reshape(8, 2, 16, 128)
    mix = a4[:, 1] + b4[:, 0]
    low = lax.broadcasted_iota(jnp.int32, (8, 16, 128), 2) < 64
    pk_out[:, 0:16, :] = jnp.where(low, a4[:, 0], mix)
    pk_out[:, 16:32, :] = jnp.where(low, mix, b4[:, 1])

    pl.semaphore_wait(barrier, expected)

    def main_copy(c):
        return remote(pk_out.at[c], pk_in.at[1 + g], enc_s.at[0, c], enc_r.at[0],
                      (c, slab_stretch))

    def carry_copy(c):
        return remote(pk_out.at[c], pk_in.at[0], enc_s.at[1, c], enc_r.at[0],
                      (c, next_stretch))

    def is_self(c, own):
        return jnp.logical_and(own, c == dp)

    def send_main(c):
        @pl.when(is_self(c, self_main))
        def _():
            local(pk_out.at[c], pk_in.at[1 + g], enc_r.at[0]).start()

        @pl.when(jnp.logical_not(is_self(c, self_main)))
        def _():
            main_copy(c).start()

    def send_carry(c):
        @pl.when(is_self(c, self_carry))
        def _():
            local(pk_out.at[c], pk_in.at[0], enc_r.at[0]).start()

        @pl.when(jnp.logical_not(is_self(c, self_carry)))
        def _():
            carry_copy(c).start()

    loop(0, 8, send_main)

    @pl.when(last_slab)
    def _():
        loop(0, 8, send_carry)

    local(valid_ref, vbuf.at[BACK + g], val_r.at[0]).start()
    loop(1, GROUP, lambda n: remote(
        valid_ref, vbuf.at[BACK + g], val_s.at[0], val_r.at[0],
        group_dev(peer(n))).start())

    arrays = ((k_ref, kb, HALO), (q_ref, qb, 0), (do_ref, dob, 0), (v_ref, vb, HALO))

    def send_head(h):
        for a, (src, buf, off) in enumerate(arrays):
            dst = buf.at[h, pl.ds(pl.multiple_of(off + g * ROWS, ROWS), ROWS)]

            def cols(p):
                return src.at[:, pl.ds(pl.multiple_of((HEADS * p + h) * DH, DH), DH)]

            local(cols(g), dst, in_r.at[h, a]).start()
            loop(0, GROUP - 1, lambda n: remote(
                cols(peer(1 + (4 * n + 1) % 7)), dst, in_s.at[h, a], in_r.at[h, a],
                group_dev(peer(1 + (4 * n + 1) % 7))).start())

    send_head(0)

    w2[0:64, :] = jnp.zeros((64, HEADS * DH), BF16)
    w2[128:192, :] = jnp.zeros((64, HEADS * DH), BF16)

    @pl.when(first)
    def _():
        kb[:, 0:HALO, :] = jnp.zeros((HEADS, HALO, DH), BF16)
        vb[:, 0:HALO, :] = jnp.zeros((HEADS, HALO, DH), BF16)
        vbuf[0:BACK] = jnp.zeros((BACK, 8, 128), jnp.int32)
        lbuf[0:BACK] = jnp.zeros((BACK, 128, 128), BF16)

    await_bytes(pk_in, enc_r.at[0])
    before = jnp.concatenate(
        [jnp.where(ctx == 0, jnp.zeros((1, 32, 128), F32), pk_in[0:1]), pk_in[1:8]], axis=0)
    x = (pk_in[1:9] + pltpu.roll(before, 64, 2)).reshape(ROWS, 128)
    lat_low = lax.broadcasted_iota(jnp.int32, (128, 128), 1) < 64
    lbuf[BACK + g] = jnp.where(lat_low, x[0:128], pltpu.roll(x[128:256], 64, 1)).astype(BF16)
    beside = g + 1 - 2 * (g % 2)

    def pass_latents(p, to, n):
        remote(lbuf.at[BACK + p], lbuf.at[BACK + p], lat_s.at[n], lat_r.at[n],
               group_dev(to)).start()

    loop(1, 4, lambda n: pass_latents(g, peer(2 * n), 0))
    pass_latents(g, beside, 2)

    send_head(1)
    send_head(2)

    await_bytes(vbuf.at[BACK:], val_r.at[0])
    halo_valid = remote(vbuf.at[pl.ds(GROUP, BACK)], vbuf.at[pl.ds(0, BACK)],
                        val_s.at[1], val_r.at[1], partner)

    @pl.when(first)
    def _():
        halo_valid.start()

    @pl.when(jnp.logical_not(first))
    def _():
        await_bytes(vbuf.at[0:BACK], val_r.at[1])

    def make_bias(s):
        rows = lax.broadcasted_iota(jnp.int32, (ROWS, 128), 0)
        ok = rows < vbuf[s, 0:1, :]
        col = jnp.where(ok, jnp.zeros((ROWS, 128), F32), jnp.full((ROWS, 128), MASKED, F32))
        at = pl.ds(pl.multiple_of(s * ROWS, ROWS), ROWS)
        bias[at, 0:128] = col
        bias[at, 128:256] = col

    loop(0, BACK + GROUP, make_bias)
    local(wlat_ref.at[:, pl.ds(0, HEADS * DH)], w2.at[pl.ds(64, 64)], loc.at[0]).wait()
    await_bytes(lbuf.at[0:3], lat_r.at[0])
    loop(1, 4, lambda n: pass_latents(peer(2 * n), beside, 2))
    await_bytes(lbuf.at[0:4], lat_r.at[2])
    halo_latents = remote(lbuf.at[pl.ds(GROUP, BACK)], lbuf.at[pl.ds(0, BACK)],
                          lat_s.at[1], lat_r.at[1], partner)

    @pl.when(first)
    def _():
        halo_latents.start()

    @pl.when(jnp.logical_not(first))
    def _():
        await_bytes(lbuf.at[0:BACK], lat_r.at[1])

    def halo_copy(h, a):
        buf = (kb, vb)[a]
        return remote(buf.at[h, pl.ds(OWN, HALO)], buf.at[h, pl.ds(0, HALO)],
                      halo_s.at[h, a], halo_r.at[h, a], partner)

    def part_copy(h):
        return remote(part_out.at[h], part_in.at[h], part_s.at[h], part_r.at[h], partner)

    def send_result(h, a, s):
        ref = (out_ref, dq_ref, dk_ref, dv_ref)[a]
        src = stg.at[a, h, pl.ds(pl.multiple_of(s * ROWS, ROWS), ROWS)]
        dst = ref.at[:, pl.ds(pl.multiple_of((HEADS * g + h) * DH, DH), DH)]

        @pl.when(s == g)
        def _():
            local(src, dst, fin_r.at[a]).start()

        @pl.when(s != g)
        def _():
            remote(src, dst, fin_s.at[h, a], fin_r.at[a], group_dev(s)).start()

    def stretch(h, i):
        rows = pl.ds(pl.multiple_of(i * ROWS, ROWS), ROWS)
        span = pl.ds(pl.multiple_of(i * ROWS, ROWS), SPAN)
        q = qb[h, rows]
        do = dob[h, rows]
        keys = kb[h, span]
        vals = vb[h, span]
        s = last_last(keys, q) + bias[span, :]
        m = jnp.max(s, axis=0, keepdims=True)
        e = jnp.exp2((s - m) * EXP2)
        p = e * (1.0 / jnp.sum(e, axis=0, keepdims=True))
        p_low = p.astype(BF16)
        out_t = first_first(vals, p_low)
        out = out_t.T.astype(BF16)
        stg[0, h, rows] = out
        delta = jnp.sum(do.astype(F32).T * out_t.astype(BF16).astype(F32), axis=0, keepdims=True)
        grad = last_last(vals, do)
        ds = (p * (grad - delta)).astype(BF16)
        stg[1, h, rows] = (first_first(keys, ds) * SCALE).T.astype(BF16)
        acc_k[h, span] += dot(ds, q)
        acc_v[h, span] += dot(p_low, do)
        send_result(h, 0, i)
        send_result(h, 1, i)

    def finish(h, s, with_part):
        rows = pl.ds(pl.multiple_of(HALO + s * ROWS, ROWS), ROWS)
        dk = acc_k[h, rows] * SCALE
        dv = acc_v[h, rows]
        if with_part:
            at = pl.ds(pl.multiple_of((s - BACK) * ROWS, ROWS), ROWS)
            dk = dk + part_in[h, 0, at].astype(F32)
            dv = dv + part_in[h, 1, at].astype(F32)
        own = pl.ds(pl.multiple_of(s * ROWS, ROWS), ROWS)
        stg[2, h, own] = dk.astype(BF16)
        stg[3, h, own] = dv.astype(BF16)

        send_result(h, 2, s)
        send_result(h, 3, s)

    def owner_of(h, j):
        return (h + j) % 2

    def owns(h):
        return xhi == owner_of(h, dp)

    def rs_copy(h, j):
        return remote(
            dwp.at[h, pl.ds(pl.multiple_of(8 * j, 8), 8)], rsb.at[h, dp * 2 + xhi],
            rs_s.at[h, j], rs_r.at[h], (j, owner_of(h, j) * GROUP + g))

    def rs_self(h, j):
        return jnp.logical_and(j == dp, owns(h))

    def own_sums(h):
        loop(0, BACK, lambda s: finish(h, s, False))

        @pl.when(jnp.logical_not(first))
        def _():
            loop(BACK, GROUP, lambda s: finish(h, s, False))

    def late_sums(h):
        @pl.when(first)
        def _():
            await_bytes(part_in.at[h], part_r.at[h])
            loop(BACK, GROUP, lambda s: finish(h, s, True))

    def share(h):
        def add(s, carry):
            top, bottom = carry
            at = pl.multiple_of(s * ROWS, ROWS)
            lat = lbuf[s]
            top = top + first_first(lat, acc_v[h, pl.ds(at, 128)].astype(BF16))
            bottom = bottom + first_first(lat, acc_v[h, pl.ds(at + 128, 128)].astype(BF16))
            return top, bottom

        zeros = jnp.zeros((128, 128), F32)
        top, bottom = lax.fori_loop(0, BACK + GROUP, add, (zeros, zeros))
        dwp[h] = top[0:64] + bottom[64:128]

        def send(j):
            @pl.when(rs_self(h, j))
            def _():
                local(dwp.at[h, pl.ds(pl.multiple_of(8 * j, 8), 8)],
                      rsb.at[h, dp * 2 + xhi], rs_r.at[h]).start()

            @pl.when(jnp.logical_not(rs_self(h, j)))
            def _():
                rs_copy(h, j).start()

        loop(0, 8, send)

    def ag_copy(h, n):
        return remote(agb.at[h, g], agb.at[h, g], ag_s.at[h], ag_r.at[h], group_dev(peer(n)))

    def add_up(h):
        @pl.when(owns(h))
        def _():
            await_bytes(rsb.at[h], rs_r.at[h])
            agb[h, g] = jnp.sum(rsb[h], axis=0)
            loop(1, GROUP, lambda n: ag_copy(h, n).start())

    def spread(h):
        @pl.when(owns(h))
        def _():
            await_bytes(agb.at[h, 0:GROUP - 1], ag_r.at[h])
            local(agb.at[h], plb.at[h * 8 + dp], pl_r.at[h]).start()
            loop(1, 16, lambda n: remote(
                agb.at[h], plb.at[h * 8 + dp], pl_s.at[h], pl_r.at[h], plane_dev(n)).start())

    def head(h):
        @pl.when(h == 2)
        def _():
            add_up(0)

        for a, (_, buf, off) in enumerate(arrays):
            await_bytes(buf.at[h, pl.ds(off, OWN)], in_r.at[h, a])

        def add_latents(s):
            lat = lbuf[BACK + s]
            at = pl.multiple_of(HALO + s * ROWS, ROWS)
            cols = pl.ds(pl.multiple_of(h * DH, DH), DH)
            upper = pl.ds(at, 128)
            lower = pl.ds(at + 128, 128)
            vb[h, upper] = (vb[h, upper].astype(F32) + dot(lat, w2[64:192, cols])).astype(BF16)
            vb[h, lower] = (vb[h, lower].astype(F32) + dot(lat, w2[0:128, cols])).astype(BF16)

        @pl.when(first)
        def _():
            halo_copy(h, 0).start()

        loop(0, GROUP, add_latents)

        @pl.when(first)
        def _():
            halo_copy(h, 1).start()

        acc_k[h] = jnp.zeros((HALO + OWN, DH), F32)
        acc_v[h] = jnp.zeros((HALO + OWN, DH), F32)

        loop(BACK, GROUP, lambda i: stretch(h, i))

        @pl.when(jnp.logical_not(first))
        def _():
            await_bytes(kb.at[h, pl.ds(0, HALO)], halo_r.at[h, 0])
            await_bytes(vb.at[h, pl.ds(0, HALO)], halo_r.at[h, 1])

        loop(0, BACK, lambda i: stretch(h, i))

        @pl.when(jnp.logical_not(first))
        def _():
            part_out[h, 0] = (acc_k[h, 0:HALO] * SCALE).astype(BF16)
            part_out[h, 1] = acc_v[h, 0:HALO].astype(BF16)
            part_copy(h).start()

        share(h)

        @pl.when(h == 0)
        def _():
            own_sums(0)

        @pl.when(h == 1)
        def _():
            late_sums(0)

    loop(0, HEADS, head)

    add_up(1)
    spread(0)
    add_up(2)
    own_sums(1)
    late_sums(1)
    own_sums(2)
    spread(1)
    spread(2)
    late_sums(2)

    def assemble(h):
        await_bytes(plb.at[pl.ds(h * 8, 8)], pl_r.at[h])
        for j in range(8):
            for p in range(GROUP):
                dw_ref[8 * j:8 * j + 8, (HEADS * p + h) * DH:(HEADS * p + h + 1) * DH] = (
                    plb[h * 8 + j, p])

    for h in range(HEADS):
        assemble(h)

    for a, ref in enumerate((out_ref, dq_ref, dk_ref, dv_ref)):
        await_bytes(ref, fin_r.at[a])

    def wait_main(c):
        @pl.when(jnp.logical_not(is_self(c, self_main)))
        def _():
            main_copy(c).wait_send()

    def wait_carry(c):
        @pl.when(jnp.logical_not(is_self(c, self_carry)))
        def _():
            carry_copy(c).wait_send()

    loop(0, 8, wait_main)

    @pl.when(last_slab)
    def _():
        loop(0, 8, wait_carry)

    await_bytes(vbuf.at[0:GROUP - 1], val_s.at[0])
    await_bytes(lbuf.at[0:3], lat_s.at[0])
    await_bytes(lbuf.at[0:4], lat_s.at[2])

    @pl.when(first)
    def _():
        await_bytes(vbuf.at[0:BACK], val_s.at[1])
        await_bytes(lbuf.at[0:BACK], lat_s.at[1])

    def drain(h):
        for a in range(4):
            await_bytes(qb.at[h, pl.ds(0, OWN - ROWS)], in_s.at[h, a])
            await_bytes(stg.at[a, h, pl.ds(0, OWN - ROWS)], fin_s.at[h, a])

        @pl.when(first)
        def _():
            await_bytes(kb.at[h, pl.ds(0, HALO)], halo_s.at[h, 0])
            await_bytes(vb.at[h, pl.ds(0, HALO)], halo_s.at[h, 1])

        @pl.when(jnp.logical_not(first))
        def _():
            await_bytes(part_out.at[h], part_s.at[h])

        def wait_rs(j):
            @pl.when(jnp.logical_not(rs_self(h, j)))
            def _():
                rs_copy(h, j).wait_send()

        loop(0, 8, wait_rs)

        @pl.when(owns(h))
        def _():
            await_bytes(agb.at[h, 0:GROUP - 1], ag_s.at[h])
            await_bytes(plb.at[0:15], pl_s.at[h])

    loop(0, HEADS, drain)


def settle(*refs):
    srcs, dsts, sem = refs[0:5], refs[5:10], refs[10]
    copies = [pltpu.make_async_copy(src, dst, sem.at[n])
              for n, (src, dst) in enumerate(zip(srcs, dsts))]
    for copy in copies:
        copy.start()
    for copy in copies:
        copy.wait()


def on_device(enc_feat, conv_w, w_lat, q_raw, k_raw, v_in, valid, d_out):
    feat = enc_feat.reshape(ROWS, enc_feat.shape[3])
    taps = conv_w.swapaxes(1, 2).reshape(-1, conv_w.shape[1])
    result = pltpu.VMEM((ROWS, q_raw.shape[2]), BF16)
    anywhere = pl.BlockSpec(memory_space=pl.ANY)
    vmem = pl.BlockSpec(memory_space=pltpu.VMEM)
    dma = pltpu.SemaphoreType.DMA
    results = pl.pallas_call(
        kernel,
        out_shape=(result, result, result, result,
                   pltpu.VMEM(w_lat.shape, F32)),
        in_specs=[vmem, vmem, vmem] + [anywhere] * 5,
        out_specs=(vmem,) * 5,
        scratch_shapes=[
            pltpu.VMEM((HEADS, OWN, DH), BF16),
            pltpu.VMEM((HEADS, OWN, DH), BF16),
            pltpu.VMEM((HEADS, HALO + OWN, DH), BF16),
            pltpu.VMEM((HEADS, HALO + OWN, DH), BF16),
            pltpu.VMEM((HEADS, HALO + OWN, DH), F32),
            pltpu.VMEM((HEADS, HALO + OWN, DH), F32),
            pltpu.VMEM((4, HEADS, OWN, DH), BF16),
            pltpu.VMEM((HEADS, 2, HALO, DH), BF16),
            pltpu.VMEM((HEADS, 2, HALO, DH), BF16),
            pltpu.VMEM((HALO + OWN, ROWS), F32),
            pltpu.VMEM((BACK + GROUP, 8, 128), jnp.int32),
            pltpu.VMEM((8, 128), jnp.int32),
            pltpu.VMEM((192, HEADS * DH), BF16),
            pltpu.VMEM((BACK + GROUP, 128, 128), BF16),
            pltpu.VMEM((8, 32, 128), F32),
            pltpu.VMEM((9, 32, 128), F32),
            pltpu.VMEM((HEADS, 64, 128), F32),
            pltpu.VMEM((HEADS, 16, 8, 128), F32),
            pltpu.VMEM((HEADS, GROUP, 8, 128), F32),
            pltpu.VMEM((HEADS * 8, GROUP, 8, 128), F32),
            dma((HEADS, 4)), dma((HEADS, 4)),
            dma((HEADS, 4)), dma((4,)),
            dma((HEADS, 2)), dma((HEADS, 2)),
            dma((HEADS,)), dma((HEADS,)),
            dma((2,)), dma((2,)),
            dma((3,)), dma((3,)),
            dma((2, 8)), dma((1,)),
            dma((HEADS, 8)), dma((HEADS,)),
            dma((HEADS,)), dma((HEADS,)),
            dma((HEADS,)), dma((HEADS,)),
            dma((1,)),
        ],
        name="slab_attention",
        compiler_params=pltpu.CompilerParams(
            collective_id=0, has_side_effects=True, vmem_limit_bytes=57 * 1024 * 1024),
    )(valid, feat, taps, w_lat, q_raw[0], k_raw[0], v_in[0], d_out[0])
    out, dq, dk, dv, dw = pl.pallas_call(
        settle,
        out_shape=tuple(jax.ShapeDtypeStruct(r.shape, r.dtype) for r in results),
        in_specs=[vmem] * 5,
        out_specs=(anywhere,) * 5,
        scratch_shapes=[dma((5,))],
        name="settle",
        compiler_params=pltpu.CompilerParams(vmem_limit_bytes=16 * 1024 * 1024),
    )(*(pltpu.with_memory_space_constraint(r, pltpu.VMEM) for r in results))
    return out[None], dq[None], dk[None], dv[None], dw


def solution(mesh):
    tokens = P("dp", "ctx", None)
    return jax.shard_map(
        on_device,
        mesh=mesh,
        in_specs=(P(None, ("dp", "ctx"), None, None), P(), P(), tokens, tokens, tokens,
                  P("dp", "ctx"), tokens),
        out_specs=(tokens, tokens, tokens, tokens, P()),
        check_vma=False,
    )
```

```python
import math

import jax
import jax.numpy as jnp
from jax import lax
from jax.experimental import pallas as pl
from jax.experimental.pallas import tpu as pltpu
from jax.sharding import PartitionSpec as P

MESH = pl.DeviceIdType.MESH
DH = 128
ROWS = 256
GROUP = 8
HEADS = 3
BACK = 4
HALO = BACK * ROWS
OWN = GROUP * ROWS
SPAN = (BACK + 1) * ROWS
SCALE = 1.0 / math.sqrt(DH)
EXP2 = SCALE * math.log2(math.e)
MASKED = -1e30
F32 = jnp.float32
BF16 = jnp.bfloat16


def last_last(a, b):
    return lax.dot_general(a, b, (((1,), (1,)), ((), ())), preferred_element_type=F32)


def first_first(a, b):
    return lax.dot_general(a, b, (((0,), (0,)), ((), ())), preferred_element_type=F32)


def dot(a, b):
    return jnp.dot(a, b, preferred_element_type=F32)


def kernel(
    count_ref, feat_ref, taps_ref, wlat_ref, q_ref, k_ref, v_ref, do_ref,
    out_ref, dq_ref, dk_ref, dv_ref, dw_ref,
    qb, dob, kb, vb, acc_k, acc_v, stg, part_out, part_in, bias, vbuf, valid_ref, w2, lbuf,
    pk_out, pk_in, dwp, rsb, agb, plb,
    in_s, in_r, fin_s, fin_r, halo_s, halo_r, part_s, part_r, val_s, val_r,
    lat_s, lat_r, enc_s, enc_r, rs_s, rs_r, ag_s, ag_r, pl_s, pl_r, loc,
):
    dp = lax.axis_index("dp")
    ctx = lax.axis_index("ctx")
    xhi = ctx // GROUP
    g = ctx % GROUP
    first = xhi == 0
    partner = (dp, ctx + GROUP - 2 * GROUP * xhi)
    slab_stretch = dp * 2 + xhi
    next_stretch = (slab_stretch + 1) % 16
    self_main = ctx == slab_stretch
    self_carry = ctx == next_stretch
    last_slab = g == GROUP - 1

    def remote(src, dst, ss, rs, dev):
        return pltpu.make_async_remote_copy(
            src_ref=src, dst_ref=dst, send_sem=ss, recv_sem=rs, device_id=dev,
            device_id_type=MESH)

    def local(src, dst, sem):
        return pltpu.make_async_copy(src, dst, sem)

    def await_bytes(ref, sem):
        pltpu.make_async_copy(ref, ref, sem).wait()

    def peer(n):
        return (g + n) % GROUP

    def group_dev(p):
        return (dp, xhi * GROUP + p)

    def loop(lo, hi, body):
        lax.fori_loop(lo, hi, lambda i, c: (body(i), c)[1], 0)

    barrier = pltpu.get_barrier_semaphore()

    def signal(dev):
        pl.semaphore_signal(barrier, inc=1, device_id=dev, device_id_type=MESH)

    loop(1, GROUP, lambda n: signal(group_dev(peer(n))))

    def plane_dev(n):
        m = (dp * 2 + xhi + n) % 16
        return (m // 2, (m % 2) * GROUP + g)

    loop(1, 16, lambda n: signal(plane_dev(n)))
    src_dp = ctx // 2
    src_ctx = (ctx % 2) * GROUP

    def signal_source(i):
        @pl.when(jnp.logical_or(src_dp != dp, src_ctx + i != ctx))
        def _():
            signal((src_dp, src_ctx + i))

    loop(0, GROUP, signal_source)
    prev = (ctx + 15) % 16
    prev_dp = prev // 2
    prev_ctx = (prev % 2) * GROUP + GROUP - 1

    @pl.when(jnp.logical_or(prev_dp != dp, prev_ctx != ctx))
    def _():
        signal((prev_dp, prev_ctx))

    one = jnp.int32(1)
    zero = jnp.int32(0)
    expected = (
        (GROUP - 1) + 15 + 8 - jnp.where(self_main, one, zero)
        + jnp.where(last_slab, 8 - jnp.where(self_carry, one, zero), zero)
    )

    local(wlat_ref.at[:, pl.ds(pl.multiple_of(g * HEADS * DH, DH), HEADS * DH)],
          w2.at[pl.ds(64, 64)], loc.at[0]).start()
    valid_ref[...] = jnp.broadcast_to(count_ref[...], (8, 128))
    a4 = last_last(feat_ref[...], taps_ref[0:128]).reshape(8, 2, 16, 128)
    b4 = last_last(feat_ref[...], taps_ref[64:192]).reshape(8, 2, 16, 128)
    mix = a4[:, 1] + b4[:, 0]
    low = lax.broadcasted_iota(jnp.int32, (8, 16, 128), 2) < 64
    pk_out[:, 0:16, :] = jnp.where(low, a4[:, 0], mix)
    pk_out[:, 16:32, :] = jnp.where(low, mix, b4[:, 1])

    pl.semaphore_wait(barrier, expected)

    def main_copy(c):
        return remote(pk_out.at[c], pk_in.at[1 + g], enc_s.at[0, c], enc_r.at[0],
                      (c, slab_stretch))

    def carry_copy(c):
        return remote(pk_out.at[c], pk_in.at[0], enc_s.at[1, c], enc_r.at[0],
                      (c, next_stretch))

    def is_self(c, own):
        return jnp.logical_and(own, c == dp)

    def send_main(c):
        @pl.when(is_self(c, self_main))
        def _():
            local(pk_out.at[c], pk_in.at[1 + g], enc_r.at[0]).start()

        @pl.when(jnp.logical_not(is_self(c, self_main)))
        def _():
            main_copy(c).start()

    def send_carry(c):
        @pl.when(is_self(c, self_carry))
        def _():
            local(pk_out.at[c], pk_in.at[0], enc_r.at[0]).start()

        @pl.when(jnp.logical_not(is_self(c, self_carry)))
        def _():
            carry_copy(c).start()

    loop(0, 8, send_main)

    @pl.when(last_slab)
    def _():
        loop(0, 8, send_carry)

    local(valid_ref, vbuf.at[BACK + g], val_r.at[0]).start()
    loop(1, GROUP, lambda n: remote(
        valid_ref, vbuf.at[BACK + g], val_s.at[0], val_r.at[0],
        group_dev(peer(n))).start())

    arrays = ((k_ref, kb, HALO), (q_ref, qb, 0), (do_ref, dob, 0), (v_ref, vb, HALO))

    def send_head(h):
        for a, (src, buf, off) in enumerate(arrays):
            dst = buf.at[h, pl.ds(pl.multiple_of(off + g * ROWS, ROWS), ROWS)]

            def cols(p):
                return src.at[:, pl.ds(pl.multiple_of((HEADS * p + h) * DH, DH), DH)]

            local(cols(g), dst, in_r.at[h, a]).start()
            loop(0, GROUP - 1, lambda n: remote(
                cols(peer(1 + (4 * n + 1) % 7)), dst, in_s.at[h, a], in_r.at[h, a],
                group_dev(peer(1 + (4 * n + 1) % 7))).start())

    send_head(0)

    w2[0:64, :] = jnp.zeros((64, HEADS * DH), BF16)
    w2[128:192, :] = jnp.zeros((64, HEADS * DH), BF16)

    @pl.when(first)
    def _():
        kb[:, 0:HALO, :] = jnp.zeros((HEADS, HALO, DH), BF16)
        vb[:, 0:HALO, :] = jnp.zeros((HEADS, HALO, DH), BF16)
        vbuf[0:BACK] = jnp.zeros((BACK, 8, 128), jnp.int32)
        lbuf[0:BACK] = jnp.zeros((BACK, 128, 128), BF16)

    await_bytes(pk_in, enc_r.at[0])
    before = jnp.concatenate(
        [jnp.where(ctx == 0, jnp.zeros((1, 32, 128), F32), pk_in[0:1]), pk_in[1:8]], axis=0)
    x = (pk_in[1:9] + pltpu.roll(before, 64, 2)).reshape(ROWS, 128)
    lat_low = lax.broadcasted_iota(jnp.int32, (128, 128), 1) < 64
    lbuf[BACK + g] = jnp.where(lat_low, x[0:128], pltpu.roll(x[128:256], 64, 1)).astype(BF16)
    beside = g + 1 - 2 * (g % 2)

    def pass_latents(p, to, n):
        remote(lbuf.at[BACK + p], lbuf.at[BACK + p], lat_s.at[n], lat_r.at[n],
               group_dev(to)).start()

    loop(1, 4, lambda n: pass_latents(g, peer(2 * n), 0))
    pass_latents(g, beside, 2)

    send_head(1)
    send_head(2)

    await_bytes(vbuf.at[BACK:], val_r.at[0])
    halo_valid = remote(vbuf.at[pl.ds(GROUP, BACK)], vbuf.at[pl.ds(0, BACK)],
                        val_s.at[1], val_r.at[1], partner)

    @pl.when(first)
    def _():
        halo_valid.start()

    @pl.when(jnp.logical_not(first))
    def _():
        await_bytes(vbuf.at[0:BACK], val_r.at[1])

    def make_bias(s):
        rows = lax.broadcasted_iota(jnp.int32, (ROWS, 128), 0)
        ok = rows < vbuf[s, 0:1, :]
        col = jnp.where(ok, jnp.zeros((ROWS, 128), F32), jnp.full((ROWS, 128), MASKED, F32))
        at = pl.ds(pl.multiple_of(s * ROWS, ROWS), ROWS)
        bias[at, 0:128] = col
        bias[at, 128:256] = col

    loop(0, BACK + GROUP, make_bias)
    local(wlat_ref.at[:, pl.ds(0, HEADS * DH)], w2.at[pl.ds(64, 64)], loc.at[0]).wait()
    await_bytes(lbuf.at[0:3], lat_r.at[0])
    loop(1, 4, lambda n: pass_latents(peer(2 * n), beside, 2))
    await_bytes(lbuf.at[0:4], lat_r.at[2])
    halo_latents = remote(lbuf.at[pl.ds(GROUP, BACK)], lbuf.at[pl.ds(0, BACK)],
                          lat_s.at[1], lat_r.at[1], partner)

    @pl.when(first)
    def _():
        halo_latents.start()

    @pl.when(jnp.logical_not(first))
    def _():
        await_bytes(lbuf.at[0:BACK], lat_r.at[1])

    def halo_copy(h, a):
        buf = (kb, vb)[a]
        return remote(buf.at[h, pl.ds(OWN, HALO)], buf.at[h, pl.ds(0, HALO)],
                      halo_s.at[h, a], halo_r.at[h, a], partner)

    def part_copy(h):
        return remote(part_out.at[h], part_in.at[h], part_s.at[h], part_r.at[h], partner)

    def send_result(h, a, s):
        ref = (out_ref, dq_ref, dk_ref, dv_ref)[a]
        src = stg.at[a, h, pl.ds(pl.multiple_of(s * ROWS, ROWS), ROWS)]
        dst = ref.at[:, pl.ds(pl.multiple_of((HEADS * g + h) * DH, DH), DH)]

        @pl.when(s == g)
        def _():
            local(src, dst, fin_r.at[a]).start()

        @pl.when(s != g)
        def _():
            remote(src, dst, fin_s.at[h, a], fin_r.at[a], group_dev(s)).start()

    def stretch(h, i):
        rows = pl.ds(pl.multiple_of(i * ROWS, ROWS), ROWS)
        span = pl.ds(pl.multiple_of(i * ROWS, ROWS), SPAN)
        q = qb[h, rows]
        do = dob[h, rows]
        keys = kb[h, span]
        vals = vb[h, span]
        s = last_last(keys, q) + bias[span, :]
        m = jnp.max(s, axis=0, keepdims=True)
        e = jnp.exp2((s - m) * EXP2)
        p = e * (1.0 / jnp.sum(e, axis=0, keepdims=True))
        p_low = p.astype(BF16)
        out_t = first_first(vals, p_low)
        out = out_t.T.astype(BF16)
        stg[0, h, rows] = out
        delta = jnp.sum(do.astype(F32).T * out_t.astype(BF16).astype(F32), axis=0, keepdims=True)
        grad = last_last(vals, do)
        ds = (p * (grad - delta)).astype(BF16)
        stg[1, h, rows] = (first_first(keys, ds) * SCALE).T.astype(BF16)
        acc_k[h, span] += dot(ds, q)
        acc_v[h, span] += dot(p_low, do)
        send_result(h, 0, i)
        send_result(h, 1, i)

    def finish(h, s, with_part):
        rows = pl.ds(pl.multiple_of(HALO + s * ROWS, ROWS), ROWS)
        dk = acc_k[h, rows] * SCALE
        dv = acc_v[h, rows]
        if with_part:
            at = pl.ds(pl.multiple_of((s - BACK) * ROWS, ROWS), ROWS)
            dk = dk + part_in[h, 0, at].astype(F32)
            dv = dv + part_in[h, 1, at].astype(F32)
        own = pl.ds(pl.multiple_of(s * ROWS, ROWS), ROWS)
        stg[2, h, own] = dk.astype(BF16)
        stg[3, h, own] = dv.astype(BF16)

        send_result(h, 2, s)
        send_result(h, 3, s)

    def owner_of(h, j):
        return (h + j) % 2

    def owns(h):
        return xhi == owner_of(h, dp)

    def rs_copy(h, j):
        return remote(
            dwp.at[h, pl.ds(pl.multiple_of(8 * j, 8), 8)], rsb.at[h, dp * 2 + xhi],
            rs_s.at[h, j], rs_r.at[h], (j, owner_of(h, j) * GROUP + g))

    def rs_self(h, j):
        return jnp.logical_and(j == dp, owns(h))

    def own_sums(h):
        loop(0, BACK, lambda s: finish(h, (s + g) % BACK, False))

        @pl.when(jnp.logical_not(first))
        def _():
            loop(0, BACK, lambda s: finish(h, BACK + (s + g) % BACK, False))

    def late_sums(h):
        @pl.when(first)
        def _():
            await_bytes(part_in.at[h], part_r.at[h])
            loop(0, BACK, lambda s: finish(h, BACK + (s + g) % BACK, True))

    def share(h):
        def add(s, carry):
            top, bottom = carry
            at = pl.multiple_of(s * ROWS, ROWS)
            lat = lbuf[s]
            top = top + first_first(lat, acc_v[h, pl.ds(at, 128)].astype(BF16))
            bottom = bottom + first_first(lat, acc_v[h, pl.ds(at + 128, 128)].astype(BF16))
            return top, bottom

        zeros = jnp.zeros((128, 128), F32)
        top, bottom = lax.fori_loop(0, BACK + GROUP, add, (zeros, zeros))
        dwp[h] = top[0:64] + bottom[64:128]

        def send(j):
            @pl.when(rs_self(h, j))
            def _():
                local(dwp.at[h, pl.ds(pl.multiple_of(8 * j, 8), 8)],
                      rsb.at[h, dp * 2 + xhi], rs_r.at[h]).start()

            @pl.when(jnp.logical_not(rs_self(h, j)))
            def _():
                rs_copy(h, j).start()

        loop(0, 8, send)

    def ag_copy(h, n):
        return remote(agb.at[h, g], agb.at[h, g], ag_s.at[h], ag_r.at[h], group_dev(peer(n)))

    def add_up(h):
        @pl.when(owns(h))
        def _():
            await_bytes(rsb.at[h], rs_r.at[h])
            agb[h, g] = jnp.sum(rsb[h], axis=0)
            loop(1, GROUP, lambda n: ag_copy(h, n).start())

    def spread(h):
        @pl.when(owns(h))
        def _():
            await_bytes(agb.at[h, 0:GROUP - 1], ag_r.at[h])
            local(agb.at[h], plb.at[h * 8 + dp], pl_r.at[h]).start()
            loop(1, 16, lambda n: remote(
                agb.at[h], plb.at[h * 8 + dp], pl_s.at[h], pl_r.at[h], plane_dev(n)).start())

    def head(h):
        @pl.when(h == 2)
        def _():
            add_up(0)

        for a, (_, buf, off) in enumerate(arrays):
            await_bytes(buf.at[h, pl.ds(off, OWN)], in_r.at[h, a])

        def add_latents(s):
            lat = lbuf[BACK + s]
            at = pl.multiple_of(HALO + s * ROWS, ROWS)
            cols = pl.ds(pl.multiple_of(h * DH, DH), DH)
            upper = pl.ds(at, 128)
            lower = pl.ds(at + 128, 128)
            vb[h, upper] = (vb[h, upper].astype(F32) + dot(lat, w2[64:192, cols])).astype(BF16)
            vb[h, lower] = (vb[h, lower].astype(F32) + dot(lat, w2[0:128, cols])).astype(BF16)

        @pl.when(first)
        def _():
            halo_copy(h, 0).start()

        loop(0, GROUP, add_latents)

        @pl.when(first)
        def _():
            halo_copy(h, 1).start()

        acc_k[h] = jnp.zeros((HALO + OWN, DH), F32)
        acc_v[h] = jnp.zeros((HALO + OWN, DH), F32)

        loop(0, BACK, lambda i: stretch(h, BACK + (i + g) % BACK))

        @pl.when(jnp.logical_not(first))
        def _():
            await_bytes(kb.at[h, pl.ds(0, HALO)], halo_r.at[h, 0])
            await_bytes(vb.at[h, pl.ds(0, HALO)], halo_r.at[h, 1])

        loop(0, BACK, lambda i: stretch(h, (i + g) % BACK))

        @pl.when(jnp.logical_not(first))
        def _():
            part_out[h, 0] = (acc_k[h, 0:HALO] * SCALE).astype(BF16)
            part_out[h, 1] = acc_v[h, 0:HALO].astype(BF16)
            part_copy(h).start()

        share(h)

        @pl.when(h == 0)
        def _():
            own_sums(0)

        @pl.when(h == 1)
        def _():
            late_sums(0)

    loop(0, HEADS, head)

    add_up(1)
    spread(0)
    add_up(2)
    own_sums(1)
    late_sums(1)
    own_sums(2)
    spread(1)
    spread(2)
    late_sums(2)

    def assemble(h):
        await_bytes(plb.at[pl.ds(h * 8, 8)], pl_r.at[h])
        for j in range(8):
            for p in range(GROUP):
                dw_ref[8 * j:8 * j + 8, (HEADS * p + h) * DH:(HEADS * p + h + 1) * DH] = (
                    plb[h * 8 + j, p])

    for h in range(HEADS):
        assemble(h)

    for a, ref in enumerate((out_ref, dq_ref, dk_ref, dv_ref)):
        await_bytes(ref, fin_r.at[a])

    def wait_main(c):
        @pl.when(jnp.logical_not(is_self(c, self_main)))
        def _():
            main_copy(c).wait_send()

    def wait_carry(c):
        @pl.when(jnp.logical_not(is_self(c, self_carry)))
        def _():
            carry_copy(c).wait_send()

    loop(0, 8, wait_main)

    @pl.when(last_slab)
    def _():
        loop(0, 8, wait_carry)

    await_bytes(vbuf.at[0:GROUP - 1], val_s.at[0])
    await_bytes(lbuf.at[0:3], lat_s.at[0])
    await_bytes(lbuf.at[0:4], lat_s.at[2])

    @pl.when(first)
    def _():
        await_bytes(vbuf.at[0:BACK], val_s.at[1])
        await_bytes(lbuf.at[0:BACK], lat_s.at[1])

    def drain(h):
        for a in range(4):
            await_bytes(qb.at[h, pl.ds(0, OWN - ROWS)], in_s.at[h, a])
            await_bytes(stg.at[a, h, pl.ds(0, OWN - ROWS)], fin_s.at[h, a])

        @pl.when(first)
        def _():
            await_bytes(kb.at[h, pl.ds(0, HALO)], halo_s.at[h, 0])
            await_bytes(vb.at[h, pl.ds(0, HALO)], halo_s.at[h, 1])

        @pl.when(jnp.logical_not(first))
        def _():
            await_bytes(part_out.at[h], part_s.at[h])

        def wait_rs(j):
            @pl.when(jnp.logical_not(rs_self(h, j)))
            def _():
                rs_copy(h, j).wait_send()

        loop(0, 8, wait_rs)

        @pl.when(owns(h))
        def _():
            await_bytes(agb.at[h, 0:GROUP - 1], ag_s.at[h])
            await_bytes(plb.at[0:15], pl_s.at[h])

    loop(0, HEADS, drain)


def settle(*refs):
    srcs, dsts, sem = refs[0:5], refs[5:10], refs[10]
    copies = [pltpu.make_async_copy(src, dst, sem.at[n])
              for n, (src, dst) in enumerate(zip(srcs, dsts))]
    for copy in copies:
        copy.start()
    for copy in copies:
        copy.wait()


def on_device(enc_feat, conv_w, w_lat, q_raw, k_raw, v_in, valid, d_out):
    feat = enc_feat.reshape(ROWS, enc_feat.shape[3])
    taps = conv_w.swapaxes(1, 2).reshape(-1, conv_w.shape[1])
    result = pltpu.VMEM((ROWS, q_raw.shape[2]), BF16)
    anywhere = pl.BlockSpec(memory_space=pl.ANY)
    vmem = pl.BlockSpec(memory_space=pltpu.VMEM)
    dma = pltpu.SemaphoreType.DMA
    results = pl.pallas_call(
        kernel,
        out_shape=(result, result, result, result,
                   pltpu.VMEM(w_lat.shape, F32)),
        in_specs=[vmem, vmem, vmem] + [anywhere] * 5,
        out_specs=(vmem,) * 5,
        scratch_shapes=[
            pltpu.VMEM((HEADS, OWN, DH), BF16),
            pltpu.VMEM((HEADS, OWN, DH), BF16),
            pltpu.VMEM((HEADS, HALO + OWN, DH), BF16),
            pltpu.VMEM((HEADS, HALO + OWN, DH), BF16),
            pltpu.VMEM((HEADS, HALO + OWN, DH), F32),
            pltpu.VMEM((HEADS, HALO + OWN, DH), F32),
            pltpu.VMEM((4, HEADS, OWN, DH), BF16),
            pltpu.VMEM((HEADS, 2, HALO, DH), BF16),
            pltpu.VMEM((HEADS, 2, HALO, DH), BF16),
            pltpu.VMEM((HALO + OWN, ROWS), F32),
            pltpu.VMEM((BACK + GROUP, 8, 128), jnp.int32),
            pltpu.VMEM((8, 128), jnp.int32),
            pltpu.VMEM((192, HEADS * DH), BF16),
            pltpu.VMEM((BACK + GROUP, 128, 128), BF16),
            pltpu.VMEM((8, 32, 128), F32),
            pltpu.VMEM((9, 32, 128), F32),
            pltpu.VMEM((HEADS, 64, 128), F32),
            pltpu.VMEM((HEADS, 16, 8, 128), F32),
            pltpu.VMEM((HEADS, GROUP, 8, 128), F32),
            pltpu.VMEM((HEADS * 8, GROUP, 8, 128), F32),
            dma((HEADS, 4)), dma((HEADS, 4)),
            dma((HEADS, 4)), dma((4,)),
            dma((HEADS, 2)), dma((HEADS, 2)),
            dma((HEADS,)), dma((HEADS,)),
            dma((2,)), dma((2,)),
            dma((3,)), dma((3,)),
            dma((2, 8)), dma((1,)),
            dma((HEADS, 8)), dma((HEADS,)),
            dma((HEADS,)), dma((HEADS,)),
            dma((HEADS,)), dma((HEADS,)),
            dma((1,)),
        ],
        name="slab_attention",
        compiler_params=pltpu.CompilerParams(
            collective_id=0, has_side_effects=True, vmem_limit_bytes=57 * 1024 * 1024),
    )(valid, feat, taps, w_lat, q_raw[0], k_raw[0], v_in[0], d_out[0])
    out, dq, dk, dv, dw = pl.pallas_call(
        settle,
        out_shape=tuple(jax.ShapeDtypeStruct(r.shape, r.dtype) for r in results),
        in_specs=[vmem] * 5,
        out_specs=(anywhere,) * 5,
        scratch_shapes=[dma((5,))],
        name="settle",
        compiler_params=pltpu.CompilerParams(vmem_limit_bytes=16 * 1024 * 1024),
    )(*(pltpu.with_memory_space_constraint(r, pltpu.VMEM) for r in results))
    return out[None], dq[None], dk[None], dv[None], dw


def solution(mesh):
    tokens = P("dp", "ctx", None)
    return jax.shard_map(
        on_device,
        mesh=mesh,
        in_specs=(P(None, ("dp", "ctx"), None, None), P(), P(), tokens, tokens, tokens,
                  P("dp", "ctx"), tokens),
        out_specs=(tokens, tokens, tokens, tokens, P()),
        check_vma=False,
    )
```
